256 devices in a mesh: span: 8 (over z), ha: 8 (over x, core), wa: 4 (over y).
Axes of the slice: x: 4, y: 4, z: 8, core: 2. Of those that a mesh axis runs over, the one named last changes fastest.
Arguments:
- queries: bfloat16 [8, 3, 32, 48, 768], P('span', None, 'ha', 'wa'), may hold values from -5 to 5
- cache_keys: bfloat16 [8, 3, 32, 48, 768], P('span', None, 'ha', 'wa'), may hold values from -5 to 5
- cache_values: bfloat16 [8, 3, 32, 48, 768], P('span', None, 'ha', 'wa'), may hold values from -16 to 16
- grad_attended: bfloat16 [8, 3, 32, 48, 768], P('span', None, 'ha', 'wa'), may hold values from -16 to 16
- radius: int32 [6], replicated, may hold values from 1 to 2, as said below
- frame_count: int32 [8], replicated, may hold values from 1 to 3, as said below
Outputs:
- attended: bfloat16 [8, 3, 32, 48, 768], P('span', None, 'ha', 'wa')
- grad_queries: bfloat16 [8, 3, 32, 48, 768], P('span', None, 'ha', 'wa')
- grad_keys: bfloat16 [8, 3, 32, 48, 768], P('span', None, 'ha', 'wa')
- grad_values: bfloat16 [8, 3, 32, 48, 768], P('span', None, 'ha', 'wa')
The draws below stay inside these ranges and needn't reach their ends.
Inputs may be any that keep to these rules, and one draw needn't show every extreme that they name: Some head has radius 2 and some other head has radius 1. Frame slots of block c at or past frame_count[c] hold padding; some block has all 3 slots live.
All inputs are finite; a program needn't handle non-finite values.
Results may differ from the reference program's by a relative error of at most 0.02.
Values may be sent and summed in bfloat16 or wider, within the bound.
A program may use at most 128 MiB of HBM per device.

```python
import math
import jax
import jax.numpy as jnp
from jax import lax

HEADS = 6
DH = 128
FR = 3
RMAX = 2
BLOCKS = 8
HT = 32
WT = 48


def paired_field(key, which):
    base = jax.random.fold_in(key, 29)
    layout = (BLOCKS, FR, HT, WT, HEADS * DH)
    first_key, second_key = jax.random.split(base, 2)
    query_part = jnp.clip(jax.random.normal(first_key, layout, jnp.float32), -4.5, 4.5)
    key_part = jnp.clip(jax.random.normal(second_key, layout, jnp.float32), -4.5, 4.5)
    if which == 0:
        return query_part.astype(jnp.bfloat16)
    return key_part.astype(jnp.bfloat16)


def draw_queries(key, part):
    return paired_field(key, 0)


def draw_cache_keys(key, part):
    return paired_field(key, 1)


def draw_radius(key, part):
    base = jax.random.fold_in(key, 41)
    first_key, second_key = jax.random.split(base)
    values = jax.random.randint(first_key, (HEADS,), 1, RMAX + 1)
    order = jax.random.permutation(second_key, HEADS)
    head_ids = jnp.arange(HEADS)
    values = jnp.where(head_ids == order[0], RMAX, values)
    values = jnp.where(head_ids == order[1], 1, values)
    return values.astype(jnp.int32)


def draw_frame_count(key, part):
    base = jax.random.fold_in(key, 53)
    first_key, second_key = jax.random.split(base)
    values = jax.random.randint(first_key, (BLOCKS,), 1, FR + 1)
    fullest = jax.random.randint(second_key, (), 0, BLOCKS)
    return jnp.where(jnp.arange(BLOCKS) == fullest, FR, values).astype(jnp.int32)


def level_of(key, shape, shards, low, largest):
    factor_of, own = 1.0, jax.random.fold_in(key, 6)
    for position, parts in shards:
        steps = jnp.exp(jax.random.uniform(jax.random.fold_in(own, position), (parts,), jnp.float32, low / len(shards), largest / len(shards)))
        factor_of = factor_of * jnp.repeat(steps, shape[position] // parts).reshape([-1 if axis == position else 1 for axis in range(len(shape))])
    return factor_of


def gaussian(own_key, extent, width, most, pieces=(), dtype=jnp.bfloat16):
    entries = jax.random.normal(own_key, extent, jnp.float32) * width
    if len(pieces) > 0:
        entries = level_of(own_key, extent, pieces, -0.22, 0.18) * entries
    return jnp.clip(entries, min=-most, max=most).astype(dtype)


def setup_inputs(seed: int = 0) -> dict:
    streams_of = jax.random.split(jax.random.key(seed), 7)
    return {
        "queries": draw_queries(jax.random.fold_in(streams_of[6], 71), 0),
        "cache_keys": draw_cache_keys(jax.random.fold_in(streams_of[6], 71), 0),
        "cache_values": gaussian(streams_of[2], (BLOCKS, FR, HT, WT, HEADS * DH), 4.0, 16.0, ((0, 8), (2, 8), (3, 4))),
        "grad_attended": gaussian(streams_of[3], (BLOCKS, FR, HT, WT, HEADS * DH), 4.0, 16.0, ((0, 8), (2, 8), (3, 4))),
        "radius": draw_radius(jax.random.fold_in(streams_of[6], 71), 0),
        "frame_count": draw_frame_count(jax.random.fold_in(streams_of[6], 71), 0),
    }


def shifted(field, along_y, along_x):
    return jnp.roll(field, (-along_y, -along_x), axis=(2, 3))

def rounded(values_f32):
    return lax.optimization_barrier(values_f32.astype(jnp.bfloat16)).astype(jnp.float32)

def reference(queries, cache_keys, cache_values, grad_attended, radius, frame_count):
    layout = (BLOCKS, FR, HT, WT, HEADS, DH)
    query_all = queries.astype(jnp.float32).reshape(layout)
    key_all = cache_keys.astype(jnp.float32).reshape(layout)
    value_all = cache_values.astype(jnp.float32).reshape(layout)
    upstream = grad_attended.astype(jnp.float32).reshape(layout)
    scale = 1.0 / math.sqrt(DH)
    block_ids = jnp.arange(BLOCKS)
    causal = block_ids[None, :] <= block_ids[:, None]
    frame_live = jnp.arange(FR)[None, :] < frame_count[:, None]
    row_ids = jnp.arange(HT)
    col_ids = jnp.arange(WT)
    offsets = [(0, 0)]
    for along_y in range(-RMAX, RMAX + 1):
        for along_x in range(-RMAX, RMAX + 1):
            if along_y != 0 or along_x != 0:
                offsets.append((along_y, along_x))

    def visible(along_y, along_x):
        inside_rows = (row_ids + along_y >= 0) & (row_ids + along_y < HT)
        inside_cols = (col_ids + along_x >= 0) & (col_ids + along_x < WT)
        inside = inside_rows[:, None] & inside_cols[None, :]
        within = radius >= max(abs(along_y), abs(along_x))
        return causal[:, None, :, None, None, None, None] & frame_live[None, None, :, :, None, None, None] & inside[None, None, None, None, :, :, None] & within[None, None, None, None, None, None, :]
    top = jnp.full((BLOCKS, FR, HT, WT, HEADS), -jnp.inf, jnp.float32)
    total = jnp.zeros((BLOCKS, FR, HT, WT, HEADS), jnp.float32)
    accum = jnp.zeros(layout, jnp.float32)
    for along_y, along_x in offsets:
        key_moved = shifted(key_all, along_y, along_x)
        value_moved = shifted(value_all, along_y, along_x)
        allowed = visible(along_y, along_x)
        score = jnp.einsum('cfyxhd,gkyxhd->cfgkyxh', query_all, key_moved) * scale
        score = jnp.where(allowed, score, -jnp.inf)
        new_top = jnp.maximum(top, lax.optimization_barrier(jnp.max(score, axis=(2, 3))))
        weight = jnp.exp(score - new_top[:, :, None, None])
        fading = jnp.exp(top - new_top)
        total = total * fading + lax.optimization_barrier(jnp.sum(weight, axis=(2, 3)))
        accum = accum * fading[..., None] + jnp.einsum('cfgkyxh,gkyxhd->cfyxhd', rounded(weight), value_moved)
        top = new_top
    attended = lax.optimization_barrier((accum / total[..., None]).astype(jnp.bfloat16))
    log_total = top + jnp.log(total)
    delta = lax.optimization_barrier(jnp.sum(upstream * attended.astype(jnp.float32), axis=-1))
    grad_q = jnp.zeros(layout, jnp.float32)
    grad_k = jnp.zeros(layout, jnp.float32)
    grad_v = jnp.zeros(layout, jnp.float32)
    for along_y, along_x in offsets:
        key_moved = shifted(key_all, along_y, along_x)
        value_moved = shifted(value_all, along_y, along_x)
        allowed = visible(along_y, along_x)
        score = jnp.einsum('cfyxhd,gkyxhd->cfgkyxh', query_all, key_moved) * scale
        prob = jnp.exp(jnp.where(allowed, score - log_total[:, :, None, None], -jnp.inf))
        grad_v = grad_v + shifted(jnp.einsum('cfgkyxh,cfyxhd->gkyxhd', rounded(prob), upstream), -along_y, -along_x)
        push = jnp.einsum('cfyxhd,gkyxhd->cfgkyxh', upstream, value_moved)
        slope = rounded(prob * (push - delta[:, :, None, None]))
        grad_q = grad_q + jnp.einsum('cfgkyxh,gkyxhd->cfyxhd', slope, key_moved)
        grad_k = grad_k + shifted(jnp.einsum('cfgkyxh,cfyxhd->gkyxhd', slope, query_all), -along_y, -along_x)
    final = (BLOCKS, FR, HT, WT, HEADS * DH)
    return (attended.reshape(final), (grad_q * scale).astype(jnp.bfloat16).reshape(final), (grad_k * scale).astype(jnp.bfloat16).reshape(final), grad_v.astype(jnp.bfloat16).reshape(final))
```

```python
import functools
import math

import jax
import jax.numpy as jnp
import numpy as np
from jax import lax
from jax.experimental import pallas as pl
from jax.experimental.pallas import tpu as pltpu
from jax.sharding import PartitionSpec as P

MESH = pl.DeviceIdType.MESH
BF = jnp.bfloat16
F32 = jnp.float32

NB = 8
NA = 8
NW = 4
FR = 3
TH = 4
TW = 12
OWN = TH * TW
WIDE = 128
DH = 128
HEADS = 6
HIDE = -1e30
SCALE = 1.0 / math.sqrt(DH)
LOG2E = math.log2(math.e)
OFFSETS = (4, 3, -3, 2, -2, 1, -1, 0)


def positions():
    order = list(range(TW)) + [-2, -1, TW, TW + 1]
    rows, cols = [], []
    for column in order:
        for row in range(TH):
            rows.append(row)
            cols.append(column)
    for first in (-2, TH):
        for column in order:
            for step in range(2):
                rows.append(first + step)
                cols.append(column)
    return np.array(rows, np.int32), np.array(cols, np.int32)


def place():
    return lax.axis_index("span"), lax.axis_index("ha"), lax.axis_index("wa")


def busy(z):
    return lax.rem(z, 4) != 3


def head_at(z):
    return z - z // 4


def at_head(h):
    return h + h // 3


def shift_up(i, n):
    return lax.rem(i + 1, n)


def shift_down(i, n):
    return lax.rem(i + n - 1, n)


def greet(z, a, w):
    barrier = pltpu.get_barrier_semaphore()
    for step in range(1, NB):
        pl.semaphore_signal(
            barrier, inc=1, device_id=(lax.rem(z + step, NB), a, w), device_id_type=MESH
        )
    for other in (shift_up(a, NA), shift_down(a, NA)):
        pl.semaphore_signal(barrier, inc=1, device_id=(z, other, w), device_id_type=MESH)
    for other in (shift_up(w, NW), shift_down(w, NW)):
        pl.semaphore_signal(barrier, inc=1, device_id=(z, a, other), device_id_type=MESH)
    pl.semaphore_wait(barrier, NB - 1 + 4)


def picker(shape, edge_dim):
    e = lax.broadcasted_iota(jnp.int32, shape, edge_dim)
    p = lax.broadcasted_iota(jnp.int32, shape, 1 - edge_dim)
    low = e & 31
    wanted = (low >> 1) * 4 + (e >> 5) * 2 + (low & 1)
    return (p == wanted).astype(F32).astype(BF)


def head_columns(h):
    return pl.ds(pl.multiple_of(h * DH, DH), DH)


def remote(src, dst, send, recv, to):
    return pltpu.make_async_remote_copy(
        src_ref=src, dst_ref=dst, send_sem=send, recv_sem=recv, device_id=to, device_id_type=MESH
    )


def gather_kernel(
    k_in, v_in, q_in, g_in, kv, qg, edge, z_send, z_recv, c_send, c_recv, r_send, r_recv
):
    z, a, w = place()
    arrays = (k_in, v_in, q_in, g_in)
    greet(z, a, w)
    pick = picker((64, 64), 0)

    def target(i, c):
        if i < 2:
            return kv.at[i, c, :, 0:OWN]
        return qg.at[i - 2, c]

    def z_copy(i, slot, t):
        return remote(
            arrays[i].at[:, :, head_columns(head_at(t))],
            target(i, z),
            z_send.at[i, slot],
            z_recv.at[i, z],
            (t, a, w),
        )

    def z_local(i):
        return pltpu.make_async_copy(
            arrays[i].at[:, :, head_columns(head_at(z))], target(i, z), z_recv.at[i, z]
        )

    def z_arrive(i, c):
        remote(target(i, c), target(i, c), z_send.at[i, 0], z_recv.at[i, c], (z, a, w)).wait_recv()

    def col_copy(side, c):
        if side == 0:
            src, dst, to = kv.at[:, c, :, 0:8], kv.at[:, c, :, 56:64], shift_down(w, NW)
        else:
            src, dst, to = kv.at[:, c, :, 40:48], kv.at[:, c, :, 48:56], shift_up(w, NW)
        return remote(src, dst, c_send.at[side, c], c_recv.at[side, c], (z, a, to))

    def row_copy(side, c):
        if side == 0:
            dst, to = kv.at[:, c, :, 96:128], shift_down(a, NA)
        else:
            dst, to = kv.at[:, c, :, 64:96], shift_up(a, NA)
        return remote(
            edge.at[side, :, c], dst, r_send.at[side, c], r_recv.at[side, c], (z, to, w)
        )

    for pair in ((0, 1), (2, 3)):
        for slot, offset in enumerate(OFFSETS):
            t = lax.rem(z + offset + NB, NB)

            @pl.when(busy(t))
            def _():
                for i in pair:
                    if offset == 0:
                        z_local(i).start()
                    else:
                        z_copy(i, slot, t).start()

    @pl.when(busy(z))
    def _():
        def cols_out(c, own):
            for i in range(2):
                if own:
                    z_local(i).wait()
                else:
                    z_arrive(i, c)
            for side in range(2):
                col_copy(side, c).start()

        def rows_out(c):
            for side in range(2):
                col_copy(side, c).wait_recv()
            for i in range(2):
                for f in range(FR):
                    out = jnp.dot(pick, kv[i, c, f, 0:64, :], preferred_element_type=F32)
                    out = out.astype(BF)
                    edge[0, i, c, f] = out[0:32]
                    edge[1, i, c, f] = out[32:64]
            for side in range(2):
                row_copy(side, c).start()

        order = (0,) + OFFSETS[:-1]
        blocks = [lax.rem(z + offset + NB, NB) for offset in order]
        for n, c in enumerate(blocks):
            cols_out(c, n == 0)
            if n > 0:
                rows_out(blocks[n - 1])
        rows_out(blocks[-1])
        for n, c in enumerate(blocks):
            for side in range(2):
                row_copy(side, c).wait_recv()
            for i in (2, 3):
                if n == 0:
                    z_local(i).wait()
                else:
                    z_arrive(i, c)
        for n, c in enumerate(blocks):
            for side in range(2):
                col_copy(side, c).wait_send()
                row_copy(side, c).wait_send()

    for slot, offset in enumerate(OFFSETS[:-1]):
        t = lax.rem(z + offset + NB, NB)

        @pl.when(busy(t))
        def _():
            for i in range(4):
                z_copy(i, slot, t).wait_send()


def nt(x, y):
    return lax.dot_general(x, y, (((1,), (1,)), ((), ())), preferred_element_type=F32)


def tn(x, y):
    return lax.dot_general(x, y, (((0,), (0,)), ((), ())), preferred_element_type=F32)


def attend_kernel(
    kv,
    qg,
    near,
    dead,
    att_out,
    dq_out,
    dk_out,
    dv_out,
    scores,
    acc,
    ad_stage,
    row_stage,
    row_in,
    col_stage,
    col_in,
    fin_stage,
    ad_send,
    ad_recv,
    fin_send,
    fin_recv,
    r_send,
    r_recv,
    c_send,
    c_recv,
):
    z, a, w = place()
    queries = FR * OWN
    keys = FR * WIDE
    ad_outs = (att_out, dq_out)
    fin_outs = (dk_out, dv_out)
    greet(z, a, w)
    spread = picker((64, 64), 1)
    me = head_at(z)

    def out_copy(outs, stage, send, recv, i, c):
        return remote(
            stage.at[i, c],
            outs[i].at[:, :, head_columns(me)],
            send.at[i, c],
            recv.at[i, me],
            (c, a, w),
        )

    def out_local(outs, stage, recv, i):
        return pltpu.make_async_copy(
            stage.at[i, z], outs[i].at[:, :, head_columns(me)], recv.at[i, me]
        )

    def out_start(outs, stage, send, recv, c):
        @pl.when(c == z)
        def _():
            for i in range(2):
                out_local(outs, stage, recv, i).start()

        @pl.when(c != z)
        def _():
            for i in range(2):
                out_copy(outs, stage, send, recv, i, c).start()

    def row_copy(side, c):
        to = shift_down(a, NA) if side == 0 else shift_up(a, NA)
        return remote(
            row_stage.at[side, :, c],
            row_in.at[side, :, c],
            r_send.at[side, c],
            r_recv.at[side, c],
            (z, to, w),
        )

    def col_copy(side, c):
        to = shift_down(w, NW) if side == 0 else shift_up(w, NW)
        return remote(
            col_stage.at[side, :, c],
            col_in.at[side, :, c],
            c_send.at[side, c],
            c_recv.at[side, c],
            (z, a, to),
        )

    def compute(c):
        query = qg[0, c].reshape(queries, DH)
        upstream = qg[1, c].reshape(queries, DH)
        near_rows = jnp.concatenate([near[...]] * FR, axis=0)

        def score_step(j, top):
            s = nt(query, kv[0, j].reshape(keys, DH))
            for f in range(FR):
                part = s[:, f * WIDE : (f + 1) * WIDE] + (near_rows + dead[pl.ds(j * FR + f, 1), :])
                scores[j, :, f * WIDE : (f + 1) * WIDE] = part
                top = jnp.maximum(top, part)
            return top

        top = lax.fori_loop(0, c + 1, score_step, jnp.full((queries, WIDE), HIDE, F32))
        top = jnp.max(top, axis=1, keepdims=True)

        def weight_step(j, carried):
            total, out = carried
            weight = jnp.exp2((scores[j] - top) * (SCALE * LOG2E))
            scores[j] = weight
            for f in range(FR):
                total = total + weight[:, f * WIDE : (f + 1) * WIDE]
            out = out + jnp.dot(
                weight.astype(BF), kv[1, j].reshape(keys, DH), preferred_element_type=F32
            )
            return total, out

        zero = jnp.zeros((queries, WIDE), F32)
        total, out = lax.fori_loop(0, c + 1, weight_step, (zero, zero))
        total = jnp.sum(total, axis=1, keepdims=True)
        attended = (out / total).astype(BF)
        delta = jnp.sum(upstream.astype(F32) * attended.astype(F32), axis=1, keepdims=True)
        ad_stage[0, c] = attended.reshape(FR, OWN, DH)
        inverse = 1.0 / total

        def grad_step(j, grad_q):
            prob = scores[j] * inverse
            push = nt(upstream, kv[1, j].reshape(keys, DH))
            slope = (prob * (push - delta)).astype(BF)
            acc[1, j] += tn(prob.astype(BF), upstream).reshape(FR, WIDE, DH)
            acc[0, j] += tn(slope, query).reshape(FR, WIDE, DH)
            return grad_q + jnp.dot(
                slope, kv[0, j].reshape(keys, DH), preferred_element_type=F32
            )

        grad_q = lax.fori_loop(0, c + 1, grad_step, zero)
        ad_stage[1, c] = (grad_q * SCALE).astype(BF).reshape(FR, OWN, DH)

    def rows_out(c):
        for i in range(2):
            for f in range(FR):
                row_stage[0, i, c, f] = acc[i, c, f, 64:96, :].astype(BF)
                row_stage[1, i, c, f] = acc[i, c, f, 96:128, :].astype(BF)
        for side in range(2):
            row_copy(side, c).start()

    def cols_out(c):
        for side in range(2):
            row_copy(side, c).wait_recv()
        for i in range(2):
            for f in range(FR):
                edge = jnp.concatenate([row_in[1, i, c, f], row_in[0, i, c, f]], axis=0)
                acc[i, c, f, 0:64, :] += jnp.dot(spread, edge, preferred_element_type=F32)
                col_stage[0, i, c, f] = acc[i, c, f, 48:56, :].astype(BF)
                col_stage[1, i, c, f] = acc[i, c, f, 56:64, :].astype(BF)
        for side in range(2):
            col_copy(side, c).start()

    def finish(c):
        for side in range(2):
            col_copy(side, c).wait_recv()
        for i in range(2):
            factor = SCALE if i == 0 else 1.0
            for f in range(FR):
                whole = acc[i, c, f, 0:OWN, :]
                left = whole[0:8] + col_in[1, i, c, f].astype(F32)
                right = whole[40:48] + col_in[0, i, c, f].astype(F32)
                whole = jnp.concatenate([left, whole[8:40], right], axis=0)
                fin_stage[i, c, f] = (whole * factor).astype(BF)
        out_start(fin_outs, fin_stage, fin_send, fin_recv, c)

    @pl.when(busy(z))
    def _():
        acc[...] = jnp.zeros_like(acc)

        def step(n, _):
            c = NB - 1 - n
            compute(c)
            out_start(ad_outs, ad_stage, ad_send, ad_recv, c)
            rows_out(c)

            @pl.when(n >= 1)
            def _():
                cols_out(c + 1)

            @pl.when(n >= 2)
            def _():
                finish(c + 2)

            return 0

        lax.fori_loop(0, NB, step, 0)
        cols_out(0)
        finish(1)
        finish(0)

        def drain(c, _):
            for side in range(2):
                row_copy(side, c).wait_send()
                col_copy(side, c).wait_send()

            @pl.when(c != z)
            def _():
                for i in range(2):
                    out_copy(ad_outs, ad_stage, ad_send, ad_recv, i, c).wait_send()
                    out_copy(fin_outs, fin_stage, fin_send, fin_recv, i, c).wait_send()

            return 0

        lax.fori_loop(0, NB, drain, 0)

    for h in range(HEADS):
        for outs, stage, send, recv in (
            (ad_outs, ad_stage, ad_send, ad_recv),
            (fin_outs, fin_stage, fin_send, fin_recv),
        ):
            for i in range(2):
                view = outs[i].at[:, :, h * DH : (h + 1) * DH]
                pltpu.make_async_copy(view, view, recv.at[i, h]).wait()


def packed(array):
    frames, tile_h, tile_w, width = array.shape[1:]
    return jnp.transpose(array[0], (0, 2, 1, 3)).reshape(frames, tile_h * tile_w, width)


def unpacked(array):
    frames, rows, width = array.shape
    return jnp.transpose(array.reshape(frames, TW, TH, width), (0, 2, 1, 3))[None]


def shards(queries, cache_keys, cache_values, grad_attended, radius, frame_count):
    z, a, w = place()
    rows, cols = positions()
    own_radius = radius[jnp.minimum(head_at(z), HEADS - 1)]
    reach = np.maximum(
        np.abs(rows[:OWN, None] - rows[None, :]), np.abs(cols[:OWN, None] - cols[None, :])
    )
    full_rows, full_cols = rows[None, :] + a * TH, cols[None, :] + w * TW
    inside = (full_rows >= 0) & (full_rows < TH * NA) & (full_cols >= 0) & (full_cols < TW * NW)
    near = jnp.where((reach <= own_radius) & inside, 0.0, HIDE).astype(F32)
    live = jnp.arange(FR)[None, :] < frame_count[:, None]
    dead = jnp.where(live.reshape(NB * FR, 1), 0.0, HIDE).astype(F32)
    dead = jnp.broadcast_to(dead, (NB * FR, WIDE))

    vmem = pl.BlockSpec(memory_space=pltpu.VMEM)
    anywhere = pl.BlockSpec(memory_space=pl.ANY)
    dma = pltpu.SemaphoreType.DMA
    kv, qg = pl.pallas_call(
        gather_kernel,
        out_shape=(
            jax.ShapeDtypeStruct((2, NB, FR, WIDE, DH), BF),
            jax.ShapeDtypeStruct((2, NB, FR, OWN, DH), BF),
        ),
        in_specs=[anywhere] * 4,
        out_specs=(vmem, vmem),
        scratch_shapes=[
            pltpu.VMEM((2, 2, NB, FR, 32, DH), BF),
            dma((4, NB)),
            dma((4, NB)),
            dma((2, NB)),
            dma((2, NB)),
            dma((2, NB)),
            dma((2, NB)),
        ],
        compiler_params=pltpu.CompilerParams(collective_id=0, has_side_effects=True),
        name="gather",
    )(packed(cache_keys), packed(cache_values), packed(queries), packed(grad_attended))

    flat = jax.ShapeDtypeStruct((FR, OWN, HEADS * DH), BF)
    outs = pl.pallas_call(
        attend_kernel,
        out_shape=(flat,) * 4,
        in_specs=[vmem] * 4,
        out_specs=(anywhere,) * 4,
        scratch_shapes=[
            pltpu.VMEM((NB, FR * OWN, FR * WIDE), F32),
            pltpu.VMEM((2, NB, FR, WIDE, DH), F32),
            pltpu.VMEM((2, NB, FR, OWN, DH), BF),
            pltpu.VMEM((2, 2, NB, FR, 32, DH), BF),
            pltpu.VMEM((2, 2, NB, FR, 32, DH), BF),
            pltpu.VMEM((2, 2, NB, FR, 8, DH), BF),
            pltpu.VMEM((2, 2, NB, FR, 8, DH), BF),
            pltpu.VMEM((2, NB, FR, OWN, DH), BF),
            dma((2, NB)),
            dma((2, NB)),
            dma((2, NB)),
            dma((2, NB)),
            dma((2, NB)),
            dma((2, NB)),
            dma((2, NB)),
            dma((2, NB)),
        ],
        compiler_params=pltpu.CompilerParams(collective_id=1, has_side_effects=True),
        name="attend",
    )(kv, qg, near, dead)
    attended, grad_queries, grad_keys, grad_values = (unpacked(x) for x in outs)
    return attended, grad_queries, grad_keys, grad_values


def solution(mesh):
    tiled = P("span", None, "ha", "wa", None)
    return jax.shard_map(
        shards,
        mesh=mesh,
        in_specs=(tiled,) * 4 + (P(), P()),
        out_specs=(tiled,) * 4,
        check_vma=False,
    )
```

```python
import math

import jax
import jax.numpy as jnp
from jax import lax
from jax.experimental import pallas as pl
from jax.experimental.pallas import tpu as pltpu
from jax.sharding import PartitionSpec as P

MESH = pl.DeviceIdType.MESH
BF = jnp.bfloat16
F32 = jnp.float32

NB = 8
NA = 8
NW = 4
FR = 3
TH = 4
TW = 12
OWN = TH * TW
WIDE = 128
DH = 128
HEADS = 6
BLOCK = FR * OWN
KEYS = FR * WIDE
GROUP = 128
HIDE = -1e30
SCALE = 1.0 / math.sqrt(DH)
LOG2E = math.log2(math.e)
OFFSETS = (4, 3, -3, 2, -2, 1, -1, 0)


def place():
    return lax.axis_index("span"), lax.axis_index("ha"), lax.axis_index("wa")


def busy(z):
    return lax.rem(z, 4) != 3


def head_at(z):
    return z - z // 4


def at_head(h):
    return h + h // 3


def shift_up(i, n):
    return lax.rem(i + 1, n)


def shift_down(i, n):
    return lax.rem(i + n - 1, n)


def greet(z, a, w):
    barrier = pltpu.get_barrier_semaphore()
    for step in range(1, NB):
        pl.semaphore_signal(
            barrier, inc=1, device_id=(lax.rem(z + step, NB), a, w), device_id_type=MESH
        )
    for other in (shift_up(a, NA), shift_down(a, NA)):
        pl.semaphore_signal(barrier, inc=1, device_id=(z, other, w), device_id_type=MESH)
    for other in (shift_up(w, NW), shift_down(w, NW)):
        pl.semaphore_signal(barrier, inc=1, device_id=(z, a, other), device_id_type=MESH)
    pl.semaphore_wait(barrier, NB - 1 + 4)


def picker(shape, edge_dim):
    e = lax.broadcasted_iota(jnp.int32, shape, edge_dim)
    p = lax.broadcasted_iota(jnp.int32, shape, 1 - edge_dim)
    low = e & 31
    wanted = (low >> 1) * 4 + (e >> 5) * 2 + (low & 1)
    return (p == wanted).astype(F32).astype(BF)


def head_columns(h):
    return pl.ds(pl.multiple_of(h * DH, DH), DH)


def remote(src, dst, send, recv, to):
    return pltpu.make_async_remote_copy(
        src_ref=src, dst_ref=dst, send_sem=send, recv_sem=recv, device_id=to, device_id_type=MESH
    )


def nt(x, y):
    return lax.dot_general(x, y, (((1,), (1,)), ((), ())), preferred_element_type=F32)


def mm(x, y):
    return jnp.dot(x, y, preferred_element_type=F32)


def arrived(view, sem):
    pltpu.make_async_copy(view, view, sem).wait()


def reach_table(near, radius, a, w):
    p = lax.broadcasted_iota(jnp.int32, (WIDE, GROUP), 0)
    lane = lax.broadcasted_iota(jnp.int32, (WIDE, GROUP), 1)
    edge = p >= 64
    low = p & 31
    column = jnp.where(edge, low >> 1, p >> 2)
    row = jnp.where(edge, (low & 1) + jnp.where(p >= 96, TH, -2), p & 3)
    column = column - jnp.where(column >= 14, 2, jnp.where(column >= 12, 14, 0))
    full_row, full_column = row + a * TH, column + w * TW
    inside = (full_row >= 0) & (full_row < TH * NA) & (full_column >= 0)
    inside = inside & (full_column < TW * NW)
    for g in range(3):
        spot = lane + (g * GROUP) % OWN
        for _ in range(3):
            spot = jnp.where(spot >= OWN, spot - OWN, spot)
        gap = jnp.maximum(jnp.abs(row - (spot & 3)), jnp.abs(column - (spot >> 2)))
        near[g] = jnp.where((gap <= radius) & inside, 0.0, HIDE).astype(F32)


def fused_kernel(
    radius,
    count,
    k_in,
    v_in,
    q_in,
    g_in,
    att_out,
    dq_out,
    dk_out,
    dv_out,
    kv,
    kvt,
    qg,
    near,
    pair,
    scores,
    pushes,
    acc,
    edge,
    ad_stage,
    row_stage,
    row_in,
    col_stage,
    col_in,
    fin_stage,
    z_send,
    z_recv,
    c_send,
    c_recv,
    r_send,
    r_recv,
    ad_send,
    ad_recv,
    fin_send,
    fin_recv,
    gr_send,
    gr_recv,
    gc_send,
    gc_recv,
):
    z, a, w = place()
    me = head_at(z)
    arrays = (k_in, v_in, q_in, g_in)
    ad_outs = (att_out, dq_out)
    fin_outs = (dk_out, dv_out)
    greet(z, a, w)

    def block_rows(c):
        return pl.ds(pl.multiple_of(c * BLOCK, 16), BLOCK)

    def target(i, c):
        if i < 2:
            return kv.at[i, c, :, 0:OWN]
        return qg.at[i - 2, block_rows(c)]

    def source(i, t):
        if i < 2:
            return arrays[i].at[:, :, head_columns(head_at(t))]
        return arrays[i].at[:, head_columns(head_at(t))]

    def z_copy(i, slot, t):
        return remote(source(i, t), target(i, z), z_send.at[i, slot], z_recv.at[i, z], (t, a, w))

    def z_local(i):
        return pltpu.make_async_copy(source(i, z), target(i, z), z_recv.at[i, z])

    def col_copy(side, c):
        if side == 0:
            src, dst, to = kv.at[:, c, :, 0:8], kv.at[:, c, :, 56:64], shift_down(w, NW)
        else:
            src, dst, to = kv.at[:, c, :, 40:48], kv.at[:, c, :, 48:56], shift_up(w, NW)
        return remote(src, dst, c_send.at[side, c], c_recv.at[side, c], (z, a, to))

    def row_copy(side, c):
        if side == 0:
            dst, to = kv.at[:, c, :, 96:128], shift_down(a, NA)
        else:
            dst, to = kv.at[:, c, :, 64:96], shift_up(a, NA)
        return remote(
            edge.at[side, :, c], dst, r_send.at[side, c], r_recv.at[side, c], (z, to, w)
        )

    for kinds in ((0, 1), (2, 3)):
        for slot, offset in enumerate(OFFSETS):
            t = lax.rem(z + offset + NB, NB)

            @pl.when(busy(t))
            def _():
                for i in kinds:
                    if offset == 0:
                        z_local(i).start()
                    else:
                        z_copy(i, slot, t).start()

    def gather():
        pick = picker((64, 64), 0)

        def cols_first(c):
            for i in range(2):
                arrived(target(i, c), z_recv.at[i, c])
            for side in range(2):
                col_copy(side, c).start()

        def rows_next(c):
            for side in range(2):
                col_copy(side, c).wait_recv()
            for i in range(2):
                for f in range(FR):
                    out = mm(pick, kv[i, c, f, 0:64, :]).astype(BF)
                    edge[0, i, c, f] = out[0:32]
                    edge[1, i, c, f] = out[32:64]
            for side in range(2):
                row_copy(side, c).start()

        def turn(c):
            for side in range(2):
                row_copy(side, c).wait_recv()
            for i in range(2):
                for f in range(FR):
                    kvt[i, c, :, f * WIDE : (f + 1) * WIDE] = kv[i, c, f].T

        order = (0,) + OFFSETS[:-1]
        blocks = [lax.rem(z + offset + NB, NB) for offset in order]
        for n in range(NB + 2):
            if n < NB:
                cols_first(blocks[n])
            if 1 <= n <= NB:
                rows_next(blocks[n - 1])
            if n >= 2:
                turn(blocks[n - 2])

    def out_copy(outs, view, send, recv, i, c):
        return remote(
            view(i, c), outs[i].at[:, head_columns(me)], send.at[i, c], recv.at[i, me], (c, a, w)
        )

    def out_start(outs, view, send, recv, c):
        @pl.when(c == z)
        def _():
            for i in range(2):
                pltpu.make_async_copy(
                    view(i, c), outs[i].at[:, head_columns(me)], recv.at[i, me]
                ).start()

        @pl.when(c != z)
        def _():
            for i in range(2):
                out_copy(outs, view, send, recv, i, c).start()

    def ad_view(i, c):
        return ad_stage.at[i, block_rows(c)]

    def fin_view(i, c):
        return fin_stage.at[i, c]

    ad = (ad_outs, ad_view, ad_send, ad_recv)
    fin = (fin_outs, fin_view, fin_send, fin_recv)

    def back_rows(side, c):
        to = shift_down(a, NA) if side == 0 else shift_up(a, NA)
        return remote(
            row_stage.at[side, :, c],
            row_in.at[side, :, c],
            gr_send.at[side, c],
            gr_recv.at[side, c],
            (z, to, w),
        )

    def back_cols(side, c):
        to = shift_down(w, NW) if side == 0 else shift_up(w, NW)
        return remote(
            col_stage.at[side, :, c],
            col_in.at[side, :, c],
            gc_send.at[side, c],
            gc_recv.at[side, c],
            (z, a, to),
        )

    def compute(g):
        rows = pl.ds(pl.multiple_of(g * GROUP, GROUP), GROUP)
        upstream = qg[1, rows, :]
        pair[0:GROUP, 0:DH] = qg[0, rows, :]
        pair[GROUP : 2 * GROUP, DH : 2 * DH] = upstream
        chunks = jnp.minimum(g, NB - 1) + 1
        lane = lax.broadcasted_iota(jnp.int32, (1, GROUP), 1)
        pattern = lax.rem(g, 3)

        def both(j):
            return jnp.concatenate(
                [kv[0, j].reshape(KEYS, DH), kv[1, j].reshape(KEYS, DH)], axis=1
            )

        def folded(x, op):
            return op(x.reshape(x.shape[0] // 8, 8, GROUP), axis=0)

        def score_step(j, top):
            r = nt(both(j), pair[...])
            causal = jnp.where(lane + (g * GROUP - j * BLOCK) >= 0, 0.0, HIDE).astype(F32)
            live = count[j]
            for f in range(FR):
                hidden = causal + jnp.where(f < live, 0.0, HIDE).astype(F32)
                part = slice(f * WIDE, (f + 1) * WIDE)
                s = r[part, 0:GROUP] + (near[pattern] + hidden)
                scores[j, part, :] = s
                top = jnp.maximum(top, folded(s, jnp.max))
            pushes[j] = r[:, GROUP:]
            return top

        top = lax.fori_loop(0, chunks, score_step, jnp.full((8, GROUP), HIDE, F32))
        top = jnp.max(top, axis=0, keepdims=True)

        def weight_step(j, carried):
            total, out = carried
            weight = jnp.exp2((scores[j] - top) * (SCALE * LOG2E))
            scores[j] = weight
            return total + folded(weight, jnp.sum), out + mm(kvt[1, j], weight.astype(BF))

        zero = jnp.zeros((DH, GROUP), F32)
        total, out = lax.fori_loop(
            0, chunks, weight_step, (jnp.zeros((8, GROUP), F32), zero)
        )
        total = jnp.sum(total, axis=0, keepdims=True)
        attended = (out / total).astype(BF)
        delta = jnp.sum(
            upstream.T.astype(F32) * attended.astype(F32), axis=0, keepdims=True
        )
        ad_stage[0, rows, :] = attended.T
        inverse = 1.0 / total

        def grad_step(j, grad_q):
            prob = scores[j] * inverse
            slope = (prob * (pushes[j] - delta)).astype(BF)
            acc[j] += mm(jnp.concatenate([slope, prob.astype(BF)], axis=1), pair[...])
            return grad_q + mm(kvt[0, j], slope)

        grad_q = lax.fori_loop(0, chunks, grad_step, zero)
        ad_stage[1, rows, :] = (grad_q * SCALE).astype(BF).T

    def part_of(i):
        return slice(i * DH, (i + 1) * DH)

    def rows_out(c):
        for i in range(2):
            for f in range(FR):
                at = f * WIDE
                row_stage[0, i, c, f] = acc[c, at + 64 : at + 96, part_of(i)].astype(BF)
                row_stage[1, i, c, f] = acc[c, at + 96 : at + 128, part_of(i)].astype(BF)
        for side in range(2):
            back_rows(side, c).start()

    def cols_out(c):
        spread = picker((64, 64), 1)
        for side in range(2):
            back_rows(side, c).wait_recv()
        for i in range(2):
            for f in range(FR):
                at = f * WIDE
                border = jnp.concatenate([row_in[1, i, c, f], row_in[0, i, c, f]], axis=0)
                acc[c, at : at + 64, part_of(i)] += mm(spread, border)
                col_stage[0, i, c, f] = acc[c, at + 48 : at + 56, part_of(i)].astype(BF)
                col_stage[1, i, c, f] = acc[c, at + 56 : at + 64, part_of(i)].astype(BF)
        for side in range(2):
            back_cols(side, c).start()

    def finish(c):
        for side in range(2):
            back_cols(side, c).wait_recv()
        for i in range(2):
            factor = SCALE if i == 0 else 1.0
            for f in range(FR):
                whole = acc[c, f * WIDE : f * WIDE + OWN, part_of(i)]
                left = whole[0:8] + col_in[1, i, c, f].astype(F32)
                right = whole[40:48] + col_in[0, i, c, f].astype(F32)
                whole = jnp.concatenate([left, whole[8:40], right], axis=0)
                fin_stage[i, c, f * OWN : (f + 1) * OWN, :] = (whole * factor).astype(BF)
        out_start(*fin, c)

    @pl.when(busy(z))
    def _():
        reach_table(near, radius[me], a, w)
        pair[...] = jnp.zeros_like(pair)
        acc[...] = jnp.zeros_like(acc)
        gather()

        def step(n, _):
            g = NB - n

            @pl.when(g >= 1)
            def _():
                for i in (2, 3):
                    arrived(target(i, g - 1), z_recv.at[i, g - 1])

            compute(g)

            @pl.when(g <= NB - 1)
            def _():
                out_start(*ad, g)
                rows_out(g)

            @pl.when(g <= NB - 2)
            def _():
                cols_out(g + 1)

            @pl.when(g <= NB - 3)
            def _():
                finish(g + 2)

            return 0

        lax.fori_loop(0, NB + 1, step, 0)
        cols_out(0)
        finish(1)
        finish(0)

        def drain(c, _):
            for side in range(2):
                col_copy(side, c).wait_send()
                row_copy(side, c).wait_send()
                back_rows(side, c).wait_send()
                back_cols(side, c).wait_send()

            @pl.when(c != z)
            def _():
                for i in range(2):
                    out_copy(*ad, i, c).wait_send()
                    out_copy(*fin, i, c).wait_send()

            return 0

        lax.fori_loop(0, NB, drain, 0)

    for slot, offset in enumerate(OFFSETS[:-1]):
        t = lax.rem(z + offset + NB, NB)

        @pl.when(busy(t))
        def _():
            for i in range(4):
                z_copy(i, slot, t).wait_send()

    for outs, _, _, recv in (ad, fin):
        for h in range(HEADS):
            for i in range(2):
                arrived(outs[i].at[:, h * DH : (h + 1) * DH], recv.at[i, h])


def packed(array):
    frames, tile_h, tile_w, width = array.shape[1:]
    return jnp.transpose(array[0], (0, 2, 1, 3)).reshape(frames, tile_h * tile_w, width)


def unpacked(array):
    width = array.shape[-1]
    return jnp.transpose(array.reshape(FR, TW, TH, width), (0, 2, 1, 3))[None]


def shards(queries, cache_keys, cache_values, grad_attended, radius, frame_count):
    smem = pl.BlockSpec(memory_space=pltpu.SMEM)
    anywhere = pl.BlockSpec(memory_space=pl.ANY)
    dma = pltpu.SemaphoreType.DMA
    flat = jax.ShapeDtypeStruct((BLOCK, HEADS * DH), BF)
    outs = pl.pallas_call(
        fused_kernel,
        out_shape=(flat,) * 4,
        in_specs=[smem] * 2 + [anywhere] * 4,
        out_specs=(anywhere,) * 4,
        scratch_shapes=[
            pltpu.VMEM((2, NB, FR, WIDE, DH), BF),
            pltpu.VMEM((2, NB, DH, KEYS), BF),
            pltpu.VMEM((2, NB * BLOCK, DH), BF),
            pltpu.VMEM((3, WIDE, GROUP), F32),
            pltpu.VMEM((2 * GROUP, 2 * DH), BF),
            pltpu.VMEM((NB, KEYS, GROUP), F32),
            pltpu.VMEM((NB, KEYS, GROUP), F32),
            pltpu.VMEM((NB, KEYS, 2 * DH), F32),
            pltpu.VMEM((2, 2, NB, FR, 32, DH), BF),
            pltpu.VMEM((2, NB * BLOCK, DH), BF),
            pltpu.VMEM((2, 2, NB, FR, 32, DH), BF),
            pltpu.VMEM((2, 2, NB, FR, 32, DH), BF),
            pltpu.VMEM((2, 2, NB, FR, 8, DH), BF),
            pltpu.VMEM((2, 2, NB, FR, 8, DH), BF),
            pltpu.VMEM((2, NB, BLOCK, DH), BF),
            dma((4, NB)),
            dma((4, NB)),
        ]
        + [dma((2, NB))] * 12,
        compiler_params=pltpu.CompilerParams(collective_id=0, has_side_effects=True),
        name="fused",
    )(
        radius,
        frame_count,
        packed(cache_keys),
        packed(cache_values),
        packed(queries).reshape(BLOCK, HEADS * DH),
        packed(grad_attended).reshape(BLOCK, HEADS * DH),
    )
    return tuple(unpacked(x) for x in outs)


def solution(mesh):
    tiled = P("span", None, "ha", "wa", None)
    return jax.shard_map(
        shards,
        mesh=mesh,
        in_specs=(tiled,) * 4 + (P(), P()),
        out_specs=(tiled,) * 4,
        check_vma=False,
    )
```

```python
import math

import jax
import jax.numpy as jnp
from jax import lax
from jax.experimental import pallas as pl
from jax.experimental.pallas import tpu as pltpu
from jax.sharding import PartitionSpec as P

MESH = pl.DeviceIdType.MESH
BF = jnp.bfloat16
F32 = jnp.float32

NB = 8
NA = 8
NW = 4
FR = 3
TH = 4
TW = 12
OWN = TH * TW
WIDE = 128
DH = 128
HEADS = 6
BLOCK = FR * OWN
KEYS = FR * WIDE
GROUP = 128
HIDE = -1e30
SCALE = 1.0 / math.sqrt(DH)
LOG2E = math.log2(math.e)
STAGES = ((1, -1), (2, -2), (3, -3), (4,))
OFFSETS = (1, -1, 2, -2, 3, -3, 4)
KEYS_VALUES = (0, 1)
QUERIES_GRADS = (2, 3)


def place():
    return lax.axis_index("span"), lax.axis_index("ha"), lax.axis_index("wa")


def busy(z):
    return lax.rem(z, 4) != 3


def head_at(z):
    return z - z // 4


def at_head(h):
    return h + h // 3


def shift_up(i, n):
    return lax.rem(i + 1, n)


def shift_down(i, n):
    return lax.rem(i + n - 1, n)


def greet(z, a, w):
    barrier = pltpu.get_barrier_semaphore()
    for step in range(1, NB):
        pl.semaphore_signal(
            barrier, inc=1, device_id=(lax.rem(z + step, NB), a, w), device_id_type=MESH
        )
    for other in (shift_up(a, NA), shift_down(a, NA)):
        pl.semaphore_signal(barrier, inc=1, device_id=(z, other, w), device_id_type=MESH)
    for other in (shift_up(w, NW), shift_down(w, NW)):
        pl.semaphore_signal(barrier, inc=1, device_id=(z, a, other), device_id_type=MESH)
    pl.semaphore_wait(barrier, NB - 1 + 4)


def picker(shape, edge_dim):
    e = lax.broadcasted_iota(jnp.int32, shape, edge_dim)
    p = lax.broadcasted_iota(jnp.int32, shape, 1 - edge_dim)
    low = e & 31
    wanted = (low >> 1) * 4 + (e >> 5) * 2 + (low & 1)
    return (p == wanted).astype(F32).astype(BF)


def head_columns(h):
    return pl.ds(pl.multiple_of(h * DH, DH), DH)


def remote(src, dst, send, recv, to):
    return pltpu.make_async_remote_copy(
        src_ref=src, dst_ref=dst, send_sem=send, recv_sem=recv, device_id=to, device_id_type=MESH
    )


def nt(x, y):
    return lax.dot_general(x, y, (((1,), (1,)), ((), ())), preferred_element_type=F32)


def mm(x, y):
    return jnp.dot(x, y, preferred_element_type=F32)


def arrived(view, sem):
    pltpu.make_async_copy(view, view, sem).wait()


def reach_table(near, radius, a, w):
    p = lax.broadcasted_iota(jnp.int32, (WIDE, GROUP), 0)
    lane = lax.broadcasted_iota(jnp.int32, (WIDE, GROUP), 1)
    edge = p >= 64
    low = p & 31
    column = jnp.where(edge, low >> 1, p >> 2)
    row = jnp.where(edge, (low & 1) + jnp.where(p >= 96, TH, -2), p & 3)
    column = column - jnp.where(column >= 14, 2, jnp.where(column >= 12, 14, 0))
    full_row, full_column = row + a * TH, column + w * TW
    inside = (full_row >= 0) & (full_row < TH * NA) & (full_column >= 0)
    inside = inside & (full_column < TW * NW)
    for g in range(3):
        spot = lane + (g * GROUP) % OWN
        for _ in range(3):
            spot = jnp.where(spot >= OWN, spot - OWN, spot)
        gap = jnp.maximum(jnp.abs(row - (spot & 3)), jnp.abs(column - (spot >> 2)))
        near[g] = jnp.where((gap <= radius) & inside, 0.0, HIDE).astype(F32)


def fused_kernel(
    radius,
    count,
    k_in,
    v_in,
    q_in,
    g_in,
    att_out,
    dq_out,
    dk_out,
    dv_out,
    wide,
    asked,
    kv,
    kvt,
    qg,
    near,
    pair,
    scores,
    pushes,
    acc,
    edge,
    ad_stage,
    row_stage,
    row_in,
    col_stage,
    col_in,
    fin_stage,
    z_send,
    z_recv,
    c_send,
    c_recv,
    r_send,
    r_recv,
    ad_send,
    ad_recv,
    fin_send,
    fin_recv,
    gr_send,
    gr_recv,
    gc_send,
    gc_recv,
):
    z, a, w = place()
    me = head_at(z)
    arrays = (k_in, v_in, q_in, g_in)
    ad_outs = (att_out, dq_out)
    fin_outs = (dk_out, dv_out)
    greet(z, a, w)

    def block_rows(c):
        return pl.ds(pl.multiple_of(c * BLOCK, 16), BLOCK)

    def target(i, c):
        if i < 2:
            return wide.at[i, c, :, 0:TW]
        return asked.at[i - 2, c]

    def source(i, t):
        return arrays[i].at[:, :, :, head_columns(head_at(t))]

    def z_copy(i, offset, t):
        slot = OFFSETS.index(offset)
        return remote(source(i, t), target(i, z), z_send.at[i, slot], z_recv.at[i, z], (t, a, w))

    def z_local(i):
        return pltpu.make_async_copy(source(i, z), target(i, z), z_recv.at[i, z])

    def z_each(kinds, offsets, act):
        for offset in offsets:
            t = lax.rem(z + offset + NB, NB)

            @pl.when(busy(t))
            def _():
                for i in kinds:
                    act(z_copy(i, offset, t))

    def z_start(kinds, offsets):
        z_each(kinds, offsets, lambda copy: copy.start())

    def z_sent(kinds, offsets):
        z_each(kinds, offsets, lambda copy: copy.wait_send())

    def col_copy(side, c):
        if side == 0:
            src, dst, to = wide.at[:, c, :, 0:2], wide.at[:, c, :, 14:16], shift_down(w, NW)
        else:
            src, dst, to = wide.at[:, c, :, 10:12], wide.at[:, c, :, 12:14], shift_up(w, NW)
        return remote(src, dst, c_send.at[side, c], c_recv.at[side, c], (z, a, to))

    def row_copy(side, c):
        if side == 0:
            dst, to = kv.at[:, c, :, 96:128], shift_down(a, NA)
        else:
            dst, to = kv.at[:, c, :, 64:96], shift_up(a, NA)
        return remote(
            edge.at[side, :, c], dst, r_send.at[side, c], r_recv.at[side, c], (z, to, w)
        )

    early = z >= NB - 2

    def first():
        @pl.when(busy(z))
        def _():
            for i in range(4):
                z_local(i).start()

        @pl.when(early)
        def _():
            z_start(QUERIES_GRADS, OFFSETS)

        z_start(KEYS_VALUES, STAGES[0])
        z_start(KEYS_VALUES, STAGES[1])

    def second():
        z_sent(KEYS_VALUES, STAGES[0])
        z_start(KEYS_VALUES, STAGES[2])

    def third():
        z_sent(KEYS_VALUES, STAGES[1])
        z_start(KEYS_VALUES, STAGES[3])

    def fourth():
        z_sent(KEYS_VALUES, STAGES[2])

        @pl.when(jnp.logical_not(early))
        def _():
            z_start(QUERIES_GRADS, OFFSETS)

    def gather():
        pick = picker((64, 64), 0)

        def cols_first(c):
            for i in range(2):
                arrived(target(i, c), z_recv.at[i, c])
            for side in range(2):
                col_copy(side, c).start()

        def rows_next(c):
            for side in range(2):
                col_copy(side, c).wait_recv()
            for i in range(2):
                for f in range(FR):
                    tile = wide[i, c, f].reshape(64, DH)
                    kv[i, c, f, 0:64, :] = tile
                    out = mm(pick, tile).astype(BF)
                    edge[0, i, c, f] = out[0:32]
                    edge[1, i, c, f] = out[32:64]
            for side in range(2):
                row_copy(side, c).start()

        def turn(c):
            for side in range(2):
                row_copy(side, c).wait_recv()
            for i in range(2):
                for f in range(FR):
                    kvt[i, c, :, f * WIDE : (f + 1) * WIDE] = kv[i, c, f].T

        steps = ((0,),) + STAGES
        later = {1: second, 2: third, 3: fourth}
        blocks = [[lax.rem(z + offset + NB, NB) for offset in step] for step in steps]
        for n in range(len(steps) + 2):
            if n < len(steps):
                if n in later:
                    later[n]()
                for c in blocks[n]:
                    cols_first(c)
            if 1 <= n <= len(steps):
                for c in blocks[n - 1]:
                    rows_next(c)
            if n >= 2:
                for c in blocks[n - 2]:
                    turn(c)

    first()

    @pl.when(jnp.logical_not(busy(z)))
    def _():
        second()
        third()
        fourth()

    def out_copy(outs, view, send, recv, i, c):
        return remote(
            view(i, c), outs[i].at[:, head_columns(me)], send.at[i, c], recv.at[i, me], (c, a, w)
        )

    def out_start(outs, view, send, recv, c):
        @pl.when(c == z)
        def _():
            for i in range(2):
                pltpu.make_async_copy(
                    view(i, c), outs[i].at[:, head_columns(me)], recv.at[i, me]
                ).start()

        @pl.when(c != z)
        def _():
            for i in range(2):
                out_copy(outs, view, send, recv, i, c).start()

    def ad_view(i, c):
        return ad_stage.at[i, block_rows(c)]

    def fin_view(i, c):
        return fin_stage.at[i, c]

    ad = (ad_outs, ad_view, ad_send, ad_recv)
    fin = (fin_outs, fin_view, fin_send, fin_recv)

    def back_rows(side, c):
        to = shift_down(a, NA) if side == 0 else shift_up(a, NA)
        return remote(
            row_stage.at[side, :, c],
            row_in.at[side, :, c],
            gr_send.at[side, c],
            gr_recv.at[side, c],
            (z, to, w),
        )

    def back_cols(side, c):
        to = shift_down(w, NW) if side == 0 else shift_up(w, NW)
        return remote(
            col_stage.at[side, :, c],
            col_in.at[side, :, c],
            gc_send.at[side, c],
            gc_recv.at[side, c],
            (z, a, to),
        )

    def compute(g):
        rows = pl.ds(pl.multiple_of(g * GROUP, GROUP), GROUP)
        upstream = qg[1, rows, :]
        pair[0:GROUP, 0:DH] = qg[0, rows, :]
        pair[GROUP : 2 * GROUP, DH : 2 * DH] = upstream
        chunks = jnp.minimum(g, NB - 1) + 1
        lane = lax.broadcasted_iota(jnp.int32, (1, GROUP), 1)
        pattern = lax.rem(g, 3)

        def both(j):
            return jnp.concatenate(
                [kv[0, j].reshape(KEYS, DH), kv[1, j].reshape(KEYS, DH)], axis=1
            )

        def folded(x, op):
            return op(x.reshape(x.shape[0] // 8, 8, GROUP), axis=0)

        def score_step(j, top):
            r = nt(both(j), pair[...])
            causal = jnp.where(lane + (g * GROUP - j * BLOCK) >= 0, 0.0, HIDE).astype(F32)
            live = count[j]
            for f in range(FR):
                hidden = causal + jnp.where(f < live, 0.0, HIDE).astype(F32)
                part = slice(f * WIDE, (f + 1) * WIDE)
                s = r[part, 0:GROUP] + (near[pattern] + hidden)
                scores[j, part, :] = s
                top = jnp.maximum(top, folded(s, jnp.max))
            pushes[j] = r[:, GROUP:]
            return top

        top = lax.fori_loop(0, chunks, score_step, jnp.full((8, GROUP), HIDE, F32))
        top = jnp.max(top, axis=0, keepdims=True)

        def weight_step(j, carried):
            total, out = carried
            weight = jnp.exp2((scores[j] - top) * (SCALE * LOG2E))
            scores[j] = weight
            return total + folded(weight, jnp.sum), out + mm(kvt[1, j], weight.astype(BF))

        zero = jnp.zeros((DH, GROUP), F32)
        total, out = lax.fori_loop(
            0, chunks, weight_step, (jnp.zeros((8, GROUP), F32), zero)
        )
        total = jnp.sum(total, axis=0, keepdims=True)
        attended = (out / total).astype(BF)
        delta = jnp.sum(
            upstream.T.astype(F32) * attended.astype(F32), axis=0, keepdims=True
        )
        ad_stage[0, rows, :] = attended.T
        inverse = 1.0 / total

        def grad_step(j, grad_q):
            prob = scores[j] * inverse
            slope = (prob * (pushes[j] - delta)).astype(BF)
            acc[j] += mm(jnp.concatenate([slope, prob.astype(BF)], axis=1), pair[...])
            return grad_q + mm(kvt[0, j], slope)

        grad_q = lax.fori_loop(0, chunks, grad_step, zero)
        ad_stage[1, rows, :] = (grad_q * SCALE).astype(BF).T

    def part_of(i):
        return slice(i * DH, (i + 1) * DH)

    def rows_out(c):
        for i in range(2):
            for f in range(FR):
                at = f * WIDE
                row_stage[0, i, c, f] = acc[c, at + 64 : at + 96, part_of(i)].astype(BF)
                row_stage[1, i, c, f] = acc[c, at + 96 : at + 128, part_of(i)].astype(BF)
        for side in range(2):
            back_rows(side, c).start()

    def cols_out(c):
        spread = picker((64, 64), 1)
        for side in range(2):
            back_rows(side, c).wait_recv()
        for i in range(2):
            for f in range(FR):
                at = f * WIDE
                border = jnp.concatenate([row_in[1, i, c, f], row_in[0, i, c, f]], axis=0)
                acc[c, at : at + 64, part_of(i)] += mm(spread, border)
                col_stage[0, i, c, f] = acc[c, at + 48 : at + 56, part_of(i)].astype(BF)
                col_stage[1, i, c, f] = acc[c, at + 56 : at + 64, part_of(i)].astype(BF)
        for side in range(2):
            back_cols(side, c).start()

    def finish(c):
        for side in range(2):
            back_cols(side, c).wait_recv()
        for i in range(2):
            factor = SCALE if i == 0 else 1.0
            for f in range(FR):
                whole = acc[c, f * WIDE : f * WIDE + OWN, part_of(i)]
                left = whole[0:8] + col_in[1, i, c, f].astype(F32)
                right = whole[40:48] + col_in[0, i, c, f].astype(F32)
                whole = jnp.concatenate([left, whole[8:40], right], axis=0)
                fin_stage[i, c, f * OWN : (f + 1) * OWN, :] = (whole * factor).astype(BF)
        out_start(*fin, c)

    @pl.when(busy(z))
    def _():
        reach_table(near, radius[me], a, w)
        pair[...] = jnp.zeros_like(pair)
        acc[...] = jnp.zeros_like(acc)
        gather()

        def step(n, _):
            g = NB - n

            @pl.when(g >= 1)
            def _():
                for i in (2, 3):
                    arrived(target(i, g - 1), z_recv.at[i, g - 1])
                    qg[i - 2, block_rows(g - 1), :] = asked[i - 2, g - 1].reshape(BLOCK, DH)

            compute(g)

            @pl.when(g <= NB - 1)
            def _():
                out_start(*ad, g)
                rows_out(g)

            @pl.when(g <= NB - 2)
            def _():
                cols_out(g + 1)

            @pl.when(g <= NB - 3)
            def _():
                finish(g + 2)

            return 0

        lax.fori_loop(0, NB + 1, step, 0)
        cols_out(0)
        finish(1)
        finish(0)

        def drain(c, _):
            for side in range(2):
                col_copy(side, c).wait_send()
                row_copy(side, c).wait_send()
                back_rows(side, c).wait_send()
                back_cols(side, c).wait_send()

            @pl.when(c != z)
            def _():
                for i in range(2):
                    out_copy(*ad, i, c).wait_send()
                    out_copy(*fin, i, c).wait_send()

            return 0

        lax.fori_loop(0, NB, drain, 0)

    z_sent(KEYS_VALUES, STAGES[3])
    z_sent(QUERIES_GRADS, OFFSETS)

    for outs, _, _, recv in (ad, fin):
        for h in range(HEADS):
            for i in range(2):
                arrived(outs[i].at[:, h * DH : (h + 1) * DH], recv.at[i, h])


def write_kernel(*refs):
    flats, tiles, flat, tile, read, write = refs[:4], refs[4:8], *refs[8:]
    reads = [pltpu.make_async_copy(flats[i], flat.at[i], read.at[i]) for i in range(4)]
    writes = [pltpu.make_async_copy(tile.at[i], tiles[i], write.at[i]) for i in range(4)]
    for copy in reads:
        copy.start()
    for i in range(4):
        reads[i].wait()
        tile[i] = flat[i].reshape(tile.shape[1:])
        writes[i].start()
    for copy in writes:
        copy.wait()


def by_columns(array):
    return jnp.transpose(array[0], (0, 2, 1, 3))


def by_rows(array):
    return jnp.transpose(array, (0, 2, 1, 3))[None]


def shards(queries, cache_keys, cache_values, grad_attended, radius, frame_count):
    smem = pl.BlockSpec(memory_space=pltpu.SMEM)
    anywhere = pl.BlockSpec(memory_space=pl.ANY)
    dma = pltpu.SemaphoreType.DMA
    flat = jax.ShapeDtypeStruct((BLOCK, HEADS * DH), BF)
    outs = pl.pallas_call(
        fused_kernel,
        out_shape=(flat,) * 4,
        in_specs=[smem] * 2 + [anywhere] * 4,
        out_specs=(anywhere,) * 4,
        scratch_shapes=[
            pltpu.VMEM((2, NB, FR, 16, TH, DH), BF),
            pltpu.VMEM((2, NB, FR, TW, TH, DH), BF),
            pltpu.VMEM((2, NB, FR, WIDE, DH), BF),
            pltpu.VMEM((2, NB, DH, KEYS), BF),
            pltpu.VMEM((2, NB * BLOCK, DH), BF),
            pltpu.VMEM((3, WIDE, GROUP), F32),
            pltpu.VMEM((2 * GROUP, 2 * DH), BF),
            pltpu.VMEM((NB, KEYS, GROUP), F32),
            pltpu.VMEM((NB, KEYS, GROUP), F32),
            pltpu.VMEM((NB, KEYS, 2 * DH), F32),
            pltpu.VMEM((2, 2, NB, FR, 32, DH), BF),
            pltpu.VMEM((2, NB * BLOCK, DH), BF),
            pltpu.VMEM((2, 2, NB, FR, 32, DH), BF),
            pltpu.VMEM((2, 2, NB, FR, 32, DH), BF),
            pltpu.VMEM((2, 2, NB, FR, 8, DH), BF),
            pltpu.VMEM((2, 2, NB, FR, 8, DH), BF),
            pltpu.VMEM((2, NB, BLOCK, DH), BF),
            dma((4, NB)),
            dma((4, NB)),
        ]
        + [dma((2, NB))] * 12,
        compiler_params=pltpu.CompilerParams(collective_id=0, has_side_effects=True),
        name="fused",
    )(
        radius,
        frame_count,
        by_columns(cache_keys),
        by_columns(cache_values),
        by_columns(queries),
        by_columns(grad_attended),
    )
    tiles = (FR, TW, TH, HEADS * DH)
    outs = pl.pallas_call(
        write_kernel,
        out_shape=(jax.ShapeDtypeStruct(tiles, BF),) * 4,
        in_specs=[anywhere] * 4,
        out_specs=(anywhere,) * 4,
        scratch_shapes=[
            pltpu.VMEM((4, BLOCK, HEADS * DH), BF),
            pltpu.VMEM((4,) + tiles, BF),
            dma((4,)),
            dma((4,)),
        ],
        name="write",
    )(*outs)
    return tuple(by_rows(x) for x in outs)


def solution(mesh):
    tiled = P("span", None, "ha", "wa", None)
    return jax.shard_map(
        shards,
        mesh=mesh,
        in_specs=(tiled,) * 4 + (P(), P()),
        out_specs=(tiled,) * 4,
        check_vma=False,
    )
```

```python
import math

import jax
import jax.numpy as jnp
from jax import lax
from jax.experimental import pallas as pl
from jax.experimental.pallas import tpu as pltpu
from jax.sharding import PartitionSpec as P

MESH = pl.DeviceIdType.MESH
BF = jnp.bfloat16
F32 = jnp.float32

NB = 8
NA = 8
NW = 4
FR = 3
TH = 4
TW = 12
OWN = TH * TW
WIDE = 128
DH = 128
HEADS = 6
BLOCK = FR * OWN
KEYS = FR * WIDE
GROUP = 128
HIDE = -1e30
SCALE = 1.0 / math.sqrt(DH)
LOG2E = math.log2(math.e)
STAGES = ((1, -1), (2, -2), (3, -3), (4,))
OFFSETS = (1, -1, 2, -2, 3, -3, 4)
KEYS_VALUES = (0, 1)
QUERIES_GRADS = (2, 3)


def place():
    return lax.axis_index("span"), lax.axis_index("ha"), lax.axis_index("wa")


def busy(z):
    return lax.rem(z, 4) != 3


def head_at(z):
    return z - z // 4


def at_head(h):
    return h + h // 3


def shift_up(i, n):
    return lax.rem(i + 1, n)


def shift_down(i, n):
    return lax.rem(i + n - 1, n)


def greet(z, a, w):
    barrier = pltpu.get_barrier_semaphore()
    for step in range(1, NB):
        pl.semaphore_signal(
            barrier, inc=1, device_id=(lax.rem(z + step, NB), a, w), device_id_type=MESH
        )
    for other in (shift_up(a, NA), shift_down(a, NA)):
        pl.semaphore_signal(barrier, inc=1, device_id=(z, other, w), device_id_type=MESH)
    for other in (shift_up(w, NW), shift_down(w, NW)):
        pl.semaphore_signal(barrier, inc=1, device_id=(z, a, other), device_id_type=MESH)
    pl.semaphore_wait(barrier, NB - 1 + 4)


def picker(shape, edge_dim):
    e = lax.broadcasted_iota(jnp.int32, shape, edge_dim)
    p = lax.broadcasted_iota(jnp.int32, shape, 1 - edge_dim)
    low = e & 31
    wanted = (low >> 1) * 4 + (e >> 5) * 2 + (low & 1)
    return (p == wanted).astype(F32).astype(BF)


def head_columns(h):
    return pl.ds(pl.multiple_of(h * DH, DH), DH)


def remote(src, dst, send, recv, to):
    return pltpu.make_async_remote_copy(
        src_ref=src, dst_ref=dst, send_sem=send, recv_sem=recv, device_id=to, device_id_type=MESH
    )


def nt(x, y):
    return lax.dot_general(x, y, (((1,), (1,)), ((), ())), preferred_element_type=F32)


def mm(x, y):
    return jnp.dot(x, y, preferred_element_type=F32)


def arrived(view, sem):
    pltpu.make_async_copy(view, view, sem).wait()


def reach_table(near, radius, a, w):
    p = lax.broadcasted_iota(jnp.int32, (WIDE, GROUP), 0)
    lane = lax.broadcasted_iota(jnp.int32, (WIDE, GROUP), 1)
    edge = p >= 64
    low = p & 31
    column = jnp.where(edge, low >> 1, p >> 2)
    row = jnp.where(edge, (low & 1) + jnp.where(p >= 96, TH, -2), p & 3)
    column = column - jnp.where(column >= 14, 2, jnp.where(column >= 12, 14, 0))
    full_row, full_column = row + a * TH, column + w * TW
    inside = (full_row >= 0) & (full_row < TH * NA) & (full_column >= 0)
    inside = inside & (full_column < TW * NW)
    for g in range(3):
        spot = lane + (g * GROUP) % OWN
        for _ in range(3):
            spot = jnp.where(spot >= OWN, spot - OWN, spot)
        gap = jnp.maximum(jnp.abs(row - (spot & 3)), jnp.abs(column - (spot >> 2)))
        near[g] = jnp.where((gap <= radius) & inside, 0.0, HIDE).astype(F32)


def fused_kernel(
    radius,
    count,
    k_in,
    v_in,
    q_in,
    g_in,
    att_out,
    dq_out,
    dk_out,
    dv_out,
    wide,
    asked,
    kv,
    kvt,
    qg,
    near,
    pair,
    scores,
    pushes,
    acc,
    edge,
    ad_stage,
    row_stage,
    row_in,
    col_stage,
    col_in,
    fin_stage,
    z_send,
    z_recv,
    c_send,
    c_recv,
    r_send,
    r_recv,
    ad_send,
    ad_recv,
    fin_send,
    fin_recv,
    gr_send,
    gr_recv,
    gc_send,
    gc_recv,
):
    z, a, w = place()
    me = head_at(z)
    arrays = (k_in, v_in, q_in, g_in)
    ad_outs = (att_out, dq_out)
    fin_outs = (dk_out, dv_out)
    greet(z, a, w)

    def block_rows(c):
        return pl.ds(pl.multiple_of(c * BLOCK, 16), BLOCK)

    def target(i, c):
        if i < 2:
            return wide.at[i, c, :, 0:TW]
        return asked.at[i - 2, c]

    def source(i, t):
        return arrays[i].at[:, :, :, head_columns(head_at(t))]

    def z_copy(i, offset, t):
        slot = OFFSETS.index(offset)
        return remote(source(i, t), target(i, z), z_send.at[i, slot], z_recv.at[i, z], (t, a, w))

    def z_local(i):
        return pltpu.make_async_copy(source(i, z), target(i, z), z_recv.at[i, z])

    def z_each(kinds, offsets, act):
        for offset in offsets:
            t = lax.rem(z + offset + NB, NB)

            @pl.when(busy(t))
            def _():
                for i in kinds:
                    act(z_copy(i, offset, t))

    def z_start(kinds, offsets):
        z_each(kinds, offsets, lambda copy: copy.start())

    def z_sent(kinds, offsets):
        z_each(kinds, offsets, lambda copy: copy.wait_send())

    def col_copy(side, c):
        if side == 0:
            src, dst, to = wide.at[:, c, :, 0:2], wide.at[:, c, :, 14:16], shift_down(w, NW)
        else:
            src, dst, to = wide.at[:, c, :, 10:12], wide.at[:, c, :, 12:14], shift_up(w, NW)
        return remote(src, dst, c_send.at[side, c], c_recv.at[side, c], (z, a, to))

    def row_copy(side, c):
        if side == 0:
            dst, to = kv.at[:, c, :, 96:128], shift_down(a, NA)
        else:
            dst, to = kv.at[:, c, :, 64:96], shift_up(a, NA)
        return remote(
            edge.at[side, :, c], dst, r_send.at[side, c], r_recv.at[side, c], (z, to, w)
        )

    early = z >= NB

    def first():
        @pl.when(busy(z))
        def _():
            for i in range(4):
                z_local(i).start()

        @pl.when(early)
        def _():
            z_start(QUERIES_GRADS, OFFSETS)

        z_start(KEYS_VALUES, STAGES[0])
        z_start(KEYS_VALUES, STAGES[1])

    def second():
        z_sent(KEYS_VALUES, STAGES[0])
        z_start(KEYS_VALUES, STAGES[2])

    def third():
        z_sent(KEYS_VALUES, STAGES[1])
        z_start(KEYS_VALUES, STAGES[3])

    def fourth():
        z_sent(KEYS_VALUES, STAGES[2])

        @pl.when(jnp.logical_not(early))
        def _():
            z_start(QUERIES_GRADS, OFFSETS)

    def gather():
        pick = picker((64, 64), 0)

        def cols_first(c):
            for i in range(2):
                arrived(target(i, c), z_recv.at[i, c])
            for side in range(2):
                col_copy(side, c).start()

        def rows_next(c):
            for side in range(2):
                col_copy(side, c).wait_recv()
            for i in range(2):
                for f in range(FR):
                    tile = wide[i, c, f].reshape(64, DH)
                    kv[i, c, f, 0:64, :] = tile
                    out = mm(pick, tile).astype(BF)
                    edge[0, i, c, f] = out[0:32]
                    edge[1, i, c, f] = out[32:64]
            for side in range(2):
                row_copy(side, c).start()

        def turn(c):
            for side in range(2):
                row_copy(side, c).wait_recv()
            for i in range(2):
                for f in range(FR):
                    kvt[i, c // 2, :, pl.ds(pl.multiple_of(lax.rem(c, 2) * KEYS + f * WIDE, WIDE), WIDE)] = kv[i, c, f].T

        steps = ((0,),) + STAGES
        later = {1: second, 2: third, 3: fourth}
        blocks = [[lax.rem(z + offset + NB, NB) for offset in step] for step in steps]
        for n in range(len(steps) + 2):
            if n < len(steps):
                if n in later:
                    later[n]()
                for c in blocks[n]:
                    cols_first(c)
            if 1 <= n <= len(steps):
                for c in blocks[n - 1]:
                    rows_next(c)
            if n >= 2:
                for c in blocks[n - 2]:
                    turn(c)

    first()

    @pl.when(jnp.logical_not(busy(z)))
    def _():
        second()
        third()
        fourth()

    def out_copy(outs, view, send, recv, i, c):
        return remote(
            view(i, c), outs[i].at[:, head_columns(me)], send.at[i, c], recv.at[i, me], (c, a, w)
        )

    def out_start(outs, view, send, recv, c):
        @pl.when(c == z)
        def _():
            for i in range(2):
                pltpu.make_async_copy(
                    view(i, c), outs[i].at[:, head_columns(me)], recv.at[i, me]
                ).start()

        @pl.when(c != z)
        def _():
            for i in range(2):
                out_copy(outs, view, send, recv, i, c).start()

    def ad_view(i, c):
        return ad_stage.at[i, block_rows(c)]

    def fin_view(i, c):
        return fin_stage.at[i, c]

    ad = (ad_outs, ad_view, ad_send, ad_recv)
    fin = (fin_outs, fin_view, fin_send, fin_recv)

    def back_rows(side, c):
        to = shift_down(a, NA) if side == 0 else shift_up(a, NA)
        return remote(
            row_stage.at[side, :, c],
            row_in.at[side, :, c],
            gr_send.at[side, c],
            gr_recv.at[side, c],
            (z, to, w),
        )

    def back_cols(side, c):
        to = shift_down(w, NW) if side == 0 else shift_up(w, NW)
        return remote(
            col_stage.at[side, :, c],
            col_in.at[side, :, c],
            gc_send.at[side, c],
            gc_recv.at[side, c],
            (z, a, to),
        )

    def compute(g):
        rows = pl.ds(pl.multiple_of(g * GROUP, GROUP), GROUP)
        upstream = qg[1, rows, :]
        pair[0:GROUP, 0:DH] = qg[0, rows, :]
        pair[GROUP : 2 * GROUP, DH : 2 * DH] = upstream
        chunks = jnp.minimum(g, NB - 1) // 2 + 1
        lane = lax.broadcasted_iota(jnp.int32, (1, GROUP), 1)
        pattern = lax.rem(g, 3)

        def both(j):
            duo = pl.ds(2 * j, 2)
            return jnp.concatenate(
                [kv[0, duo].reshape(2 * KEYS, DH), kv[1, duo].reshape(2 * KEYS, DH)], axis=1
            )

        def folded(x, op):
            return op(x.reshape(x.shape[0] // 8, 8, GROUP), axis=0)

        def score_step(j, top):
            r = nt(both(j), pair[...])
            for b in range(2):
                block = 2 * j + b
                causal = jnp.where(lane + (g * GROUP - block * BLOCK) >= 0, 0.0, HIDE).astype(F32)
                live = count[block]
                for f in range(FR):
                    hidden = causal + jnp.where(f < live, 0.0, HIDE).astype(F32)
                    part = slice((b * FR + f) * WIDE, (b * FR + f + 1) * WIDE)
                    s = r[part, 0:GROUP] + (near[pattern] + hidden)
                    scores[j, part, :] = s
                    top = jnp.maximum(top, folded(s, jnp.max))
            pushes[j] = r[:, GROUP:]
            return top

        top = lax.fori_loop(0, chunks, score_step, jnp.full((8, GROUP), HIDE, F32))
        top = jnp.max(top, axis=0, keepdims=True)

        def weight_step(j, carried):
            total, out = carried
            weight = jnp.exp2((scores[j] - top) * (SCALE * LOG2E))
            scores[j] = weight
            return total + folded(weight, jnp.sum), out + mm(kvt[1, j], weight.astype(BF))

        zero = jnp.zeros((DH, GROUP), F32)
        total, out = lax.fori_loop(
            0, chunks, weight_step, (jnp.zeros((8, GROUP), F32), zero)
        )
        total = jnp.sum(total, axis=0, keepdims=True)
        attended = (out / total).astype(BF)
        delta = jnp.sum(
            upstream.T.astype(F32) * attended.astype(F32), axis=0, keepdims=True
        )
        ad_stage[0, rows, :] = attended.T
        inverse = 1.0 / total

        def grad_step(j, grad_q):
            prob = scores[j] * inverse
            slope = (prob * (pushes[j] - delta)).astype(BF)
            acc[j] += mm(jnp.concatenate([slope, prob.astype(BF)], axis=1), pair[...])
            return grad_q + mm(kvt[0, j], slope)

        grad_q = lax.fori_loop(0, chunks, grad_step, zero)
        ad_stage[1, rows, :] = (grad_q * SCALE).astype(BF).T

    def part_of(i):
        return slice(i * DH, (i + 1) * DH)

    def spot(at, low, high):
        return pl.ds(pl.multiple_of(at + low, 8), high - low)

    def rows_out(c):
        for i in range(2):
            for f in range(FR):
                at = lax.rem(c, 2) * KEYS + f * WIDE
                row_stage[0, i, c, f] = acc[c // 2, spot(at, 64, 96), part_of(i)].astype(BF)
                row_stage[1, i, c, f] = acc[c // 2, spot(at, 96, 128), part_of(i)].astype(BF)
        for side in range(2):
            back_rows(side, c).start()

    def cols_out(c):
        spread = picker((64, 64), 1)
        for side in range(2):
            back_rows(side, c).wait_recv()
        for i in range(2):
            for f in range(FR):
                at = lax.rem(c, 2) * KEYS + f * WIDE
                border = jnp.concatenate([row_in[1, i, c, f], row_in[0, i, c, f]], axis=0)
                acc[c // 2, spot(at, 0, 64), part_of(i)] += mm(spread, border)
                col_stage[0, i, c, f] = acc[c // 2, spot(at, 48, 56), part_of(i)].astype(BF)
                col_stage[1, i, c, f] = acc[c // 2, spot(at, 56, 64), part_of(i)].astype(BF)
        for side in range(2):
            back_cols(side, c).start()

    def finish(c):
        for side in range(2):
            back_cols(side, c).wait_recv()
        for i in range(2):
            factor = SCALE if i == 0 else 1.0
            for f in range(FR):
                whole = acc[c // 2, spot(lax.rem(c, 2) * KEYS + f * WIDE, 0, OWN), part_of(i)]
                left = whole[0:8] + col_in[1, i, c, f].astype(F32)
                right = whole[40:48] + col_in[0, i, c, f].astype(F32)
                whole = jnp.concatenate([left, whole[8:40], right], axis=0)
                fin_stage[i, c, f * OWN : (f + 1) * OWN, :] = (whole * factor).astype(BF)
        out_start(*fin, c)

    @pl.when(busy(z))
    def _():
        reach_table(near, radius[me], a, w)
        pair[...] = jnp.zeros_like(pair)
        acc[...] = jnp.zeros_like(acc)
        gather()

        def step(n, _):
            g = NB - n

            @pl.when(g >= 1)
            def _():
                for i in (2, 3):
                    arrived(target(i, g - 1), z_recv.at[i, g - 1])
                    qg[i - 2, block_rows(g - 1), :] = asked[i - 2, g - 1].reshape(BLOCK, DH)

            compute(g)

            @pl.when(g <= NB - 1)
            def _():
                out_start(*ad, g)
                rows_out(g)

            @pl.when(g <= NB - 2)
            def _():
                cols_out(g + 1)

            @pl.when(g <= NB - 3)
            def _():
                finish(g + 2)

            return 0

        lax.fori_loop(0, NB + 1, step, 0)
        cols_out(0)
        finish(1)
        finish(0)

        def drain(c, _):
            for side in range(2):
                col_copy(side, c).wait_send()
                row_copy(side, c).wait_send()
                back_rows(side, c).wait_send()
                back_cols(side, c).wait_send()

            @pl.when(c != z)
            def _():
                for i in range(2):
                    out_copy(*ad, i, c).wait_send()
                    out_copy(*fin, i, c).wait_send()

            return 0

        lax.fori_loop(0, NB, drain, 0)

    z_sent(KEYS_VALUES, STAGES[3])
    z_sent(QUERIES_GRADS, OFFSETS)

    for outs, _, _, recv in (ad, fin):
        for h in range(HEADS):
            for i in range(2):
                arrived(outs[i].at[:, h * DH : (h + 1) * DH], recv.at[i, h])


def write_kernel(*refs):
    flats, tiles, flat, tile, read, write = refs[:4], refs[4:8], *refs[8:]
    reads = [pltpu.make_async_copy(flats[i], flat.at[i], read.at[i]) for i in range(4)]
    writes = [pltpu.make_async_copy(tile.at[i], tiles[i], write.at[i]) for i in range(4)]
    for copy in reads:
        copy.start()
    for i in range(4):
        reads[i].wait()
        tile[i] = flat[i].reshape(tile.shape[1:])
        writes[i].start()
    for copy in writes:
        copy.wait()


def by_columns(array):
    return jnp.transpose(array[0], (0, 2, 1, 3))


def by_rows(array):
    return jnp.transpose(array, (0, 2, 1, 3))[None]


def shards(queries, cache_keys, cache_values, grad_attended, radius, frame_count):
    smem = pl.BlockSpec(memory_space=pltpu.SMEM)
    anywhere = pl.BlockSpec(memory_space=pl.ANY)
    dma = pltpu.SemaphoreType.DMA
    flat = jax.ShapeDtypeStruct((BLOCK, HEADS * DH), BF)
    outs = pl.pallas_call(
        fused_kernel,
        out_shape=(flat,) * 4,
        in_specs=[smem] * 2 + [anywhere] * 4,
        out_specs=(anywhere,) * 4,
        scratch_shapes=[
            pltpu.VMEM((2, NB, FR, 16, TH, DH), BF),
            pltpu.VMEM((2, NB, FR, TW, TH, DH), BF),
            pltpu.VMEM((2, NB, FR, WIDE, DH), BF),
            pltpu.VMEM((2, NB // 2, DH, 2 * KEYS), BF),
            pltpu.VMEM((2, NB * BLOCK, DH), BF),
            pltpu.VMEM((3, WIDE, GROUP), F32),
            pltpu.VMEM((2 * GROUP, 2 * DH), BF),
            pltpu.VMEM((NB // 2, 2 * KEYS, GROUP), F32),
            pltpu.VMEM((NB // 2, 2 * KEYS, GROUP), F32),
            pltpu.VMEM((NB // 2, 2 * KEYS, 2 * DH), F32),
            pltpu.VMEM((2, 2, NB, FR, 32, DH), BF),
            pltpu.VMEM((2, NB * BLOCK, DH), BF),
            pltpu.VMEM((2, 2, NB, FR, 32, DH), BF),
            pltpu.VMEM((2, 2, NB, FR, 32, DH), BF),
            pltpu.VMEM((2, 2, NB, FR, 8, DH), BF),
            pltpu.VMEM((2, 2, NB, FR, 8, DH), BF),
            pltpu.VMEM((2, NB, BLOCK, DH), BF),
            dma((4, NB)),
            dma((4, NB)),
        ]
        + [dma((2, NB))] * 12,
        compiler_params=pltpu.CompilerParams(collective_id=0, has_side_effects=True),
        name="fused",
    )(
        radius,
        frame_count,
        by_columns(cache_keys),
        by_columns(cache_values),
        by_columns(queries),
        by_columns(grad_attended),
    )
    tiles = (FR, TW, TH, HEADS * DH)
    outs = pl.pallas_call(
        write_kernel,
        out_shape=(jax.ShapeDtypeStruct(tiles, BF),) * 4,
        in_specs=[anywhere] * 4,
        out_specs=(anywhere,) * 4,
        scratch_shapes=[
            pltpu.VMEM((4, BLOCK, HEADS * DH), BF),
            pltpu.VMEM((4,) + tiles, BF),
            dma((4,)),
            dma((4,)),
        ],
        name="write",
    )(*outs)
    return tuple(by_rows(x) for x in outs)


def solution(mesh):
    tiled = P("span", None, "ha", "wa", None)
    return jax.shard_map(
        shards,
        mesh=mesh,
        in_specs=(tiled,) * 4 + (P(), P()),
        out_specs=(tiled,) * 4,
        check_vma=False,
    )
```

```python
import math

import jax
import jax.numpy as jnp
from jax import lax
from jax.experimental import pallas as pl
from jax.experimental.pallas import tpu as pltpu
from jax.sharding import PartitionSpec as P

MESH = pl.DeviceIdType.MESH
BF = jnp.bfloat16
F32 = jnp.float32

NB = 8
NA = 8
NW = 4
FR = 3
TH = 4
TW = 12
OWN = TH * TW
WIDE = 128
DH = 128
HEADS = 6
BLOCK = FR * OWN
KEYS = FR * WIDE
GROUP = 128
HIDE = -1e30
SCALE = 1.0 / math.sqrt(DH)
LOG2E = math.log2(math.e)
STAGES = ((4, 1, -1), (3, -3), (2, -2), ())
OFFSETS = (1, -1, 2, -2, 3, -3, 4)
KEYS_VALUES = (0, 1)
QUERIES_GRADS = (2, 3)


def place():
    return lax.axis_index("span"), lax.axis_index("ha"), lax.axis_index("wa")


def busy(z):
    return lax.rem(z, 4) != 3


def head_at(z):
    return z - z // 4


def at_head(h):
    return h + h // 3


def shift_up(i, n):
    return lax.rem(i + 1, n)


def shift_down(i, n):
    return lax.rem(i + n - 1, n)


def greet(z, a, w):
    barrier = pltpu.get_barrier_semaphore()
    for step in range(1, NB):
        pl.semaphore_signal(
            barrier, inc=1, device_id=(lax.rem(z + step, NB), a, w), device_id_type=MESH
        )
    for other in (shift_up(a, NA), shift_down(a, NA)):
        pl.semaphore_signal(barrier, inc=1, device_id=(z, other, w), device_id_type=MESH)
    for other in (shift_up(w, NW), shift_down(w, NW)):
        pl.semaphore_signal(barrier, inc=1, device_id=(z, a, other), device_id_type=MESH)
    pl.semaphore_wait(barrier, NB - 1 + 4)


def picker(shape, edge_dim):
    e = lax.broadcasted_iota(jnp.int32, shape, edge_dim)
    p = lax.broadcasted_iota(jnp.int32, shape, 1 - edge_dim)
    low = e & 31
    wanted = (low >> 1) * 4 + (e >> 5) * 2 + (low & 1)
    return (p == wanted).astype(F32).astype(BF)


def head_columns(h):
    return pl.ds(pl.multiple_of(h * DH, DH), DH)


def remote(src, dst, send, recv, to):
    return pltpu.make_async_remote_copy(
        src_ref=src, dst_ref=dst, send_sem=send, recv_sem=recv, device_id=to, device_id_type=MESH
    )


def nt(x, y):
    return lax.dot_general(x, y, (((1,), (1,)), ((), ())), preferred_element_type=F32)


def mm(x, y):
    return jnp.dot(x, y, preferred_element_type=F32)


def arrived(view, sem):
    pltpu.make_async_copy(view, view, sem).wait()


def reach_table(near, radius, a, w):
    p = lax.broadcasted_iota(jnp.int32, (WIDE, GROUP), 0)
    lane = lax.broadcasted_iota(jnp.int32, (WIDE, GROUP), 1)
    edge = p >= 64
    low = p & 31
    column = jnp.where(edge, low >> 1, p >> 2)
    row = jnp.where(edge, (low & 1) + jnp.where(p >= 96, TH, -2), p & 3)
    column = column - jnp.where(column >= 14, 2, jnp.where(column >= 12, 14, 0))
    full_row, full_column = row + a * TH, column + w * TW
    inside = (full_row >= 0) & (full_row < TH * NA) & (full_column >= 0)
    inside = inside & (full_column < TW * NW)
    for g in range(3):
        spot = lane + (g * GROUP) % OWN
        for _ in range(3):
            spot = jnp.where(spot >= OWN, spot - OWN, spot)
        gap = jnp.maximum(jnp.abs(row - (spot & 3)), jnp.abs(column - (spot >> 2)))
        near[g] = jnp.where((gap <= radius) & inside, 0.0, HIDE).astype(F32)


def fused_kernel(
    radius,
    count,
    k_in,
    v_in,
    q_in,
    g_in,
    att_out,
    dq_out,
    dk_out,
    dv_out,
    wide,
    asked,
    kv,
    kvt,
    qg,
    near,
    pair,
    scores,
    pushes,
    acc,
    edge,
    ad_stage,
    row_stage,
    row_in,
    col_stage,
    col_in,
    fin_stage,
    z_send,
    z_recv,
    c_send,
    c_recv,
    r_send,
    r_recv,
    ad_send,
    ad_recv,
    fin_send,
    fin_recv,
    gr_send,
    gr_recv,
    gc_send,
    gc_recv,
):
    z, a, w = place()
    me = head_at(z)
    arrays = (k_in, v_in, q_in, g_in)
    ad_outs = (att_out, dq_out)
    fin_outs = (dk_out, dv_out)
    greet(z, a, w)

    def block_rows(c):
        return pl.ds(pl.multiple_of(c * BLOCK, 16), BLOCK)

    def target(i, c):
        if i < 2:
            return wide.at[i, c, :, 0:TW]
        return asked.at[i - 2, c]

    def source(i, t):
        return arrays[i].at[:, :, :, head_columns(head_at(t))]

    def z_copy(i, offset, t):
        slot = OFFSETS.index(offset)
        return remote(source(i, t), target(i, z), z_send.at[i, slot], z_recv.at[i, z], (t, a, w))

    def z_local(i):
        return pltpu.make_async_copy(source(i, z), target(i, z), z_recv.at[i, z])

    def z_each(kinds, offsets, act):
        for offset in offsets:
            t = lax.rem(z + offset + NB, NB)

            @pl.when(busy(t))
            def _():
                for i in kinds:
                    act(z_copy(i, offset, t))

    def z_start(kinds, offsets):
        z_each(kinds, offsets, lambda copy: copy.start())

    def z_sent(kinds, offsets):
        z_each(kinds, offsets, lambda copy: copy.wait_send())

    def col_copy(side, c):
        if side == 0:
            src, dst, to = wide.at[:, c, :, 0:2], wide.at[:, c, :, 14:16], shift_down(w, NW)
        else:
            src, dst, to = wide.at[:, c, :, 10:12], wide.at[:, c, :, 12:14], shift_up(w, NW)
        return remote(src, dst, c_send.at[side, c], c_recv.at[side, c], (z, a, to))

    def row_copy(side, c):
        if side == 0:
            dst, to = kv.at[:, c, :, 96:128], shift_down(a, NA)
        else:
            dst, to = kv.at[:, c, :, 64:96], shift_up(a, NA)
        return remote(
            edge.at[side, :, c], dst, r_send.at[side, c], r_recv.at[side, c], (z, to, w)
        )

    upper = z >= NB // 2

    def first():
        @pl.when(busy(z))
        def _():
            for i in range(4):
                z_local(i).start()

        z_start(KEYS_VALUES, STAGES[0])
        z_start(KEYS_VALUES, STAGES[1])

    def second():
        z_sent(KEYS_VALUES, STAGES[0])
        z_start(KEYS_VALUES, STAGES[2])

    def third():
        z_sent(KEYS_VALUES, STAGES[1])
        z_start(KEYS_VALUES, STAGES[3])

    def fourth():
        z_sent(KEYS_VALUES, STAGES[2])

        @pl.when(upper)
        def _():
            z_start(QUERIES_GRADS, OFFSETS)

    def fifth():
        @pl.when(jnp.logical_not(upper))
        def _():
            z_start(QUERIES_GRADS, OFFSETS)

    def gather():
        pick = picker((64, 64), 0)

        def cols_first(c):
            for i in range(2):
                arrived(target(i, c), z_recv.at[i, c])
            for side in range(2):
                col_copy(side, c).start()

        def rows_next(c):
            for side in range(2):
                col_copy(side, c).wait_recv()
            for i in range(2):
                for f in range(FR):
                    tile = wide[i, c, f].reshape(64, DH)
                    kv[i, c, f, 0:64, :] = tile
                    out = mm(pick, tile).astype(BF)
                    edge[0, i, c, f] = out[0:32]
                    edge[1, i, c, f] = out[32:64]
            for side in range(2):
                row_copy(side, c).start()

        def turn(c):
            for side in range(2):
                row_copy(side, c).wait_recv()
            for i in range(2):
                for f in range(FR):
                    kvt[i, c // 2, :, pl.ds(pl.multiple_of(lax.rem(c, 2) * KEYS + f * WIDE, WIDE), WIDE)] = kv[i, c, f].T

        steps = ((0,),) + STAGES
        later = {1: second, 2: third, 3: fourth}
        blocks = [[lax.rem(z + offset + NB, NB) for offset in step] for step in steps]
        for n in range(len(steps) + 2):
            if n < len(steps):
                if n in later:
                    later[n]()
                for c in blocks[n]:
                    cols_first(c)
            if 1 <= n <= len(steps):
                for c in blocks[n - 1]:
                    rows_next(c)
            if n >= 2:
                for c in blocks[n - 2]:
                    turn(c)

    first()

    @pl.when(jnp.logical_not(busy(z)))
    def _():
        second()
        third()
        fourth()
        z_sent(KEYS_VALUES, STAGES[3])
        fifth()

    def out_copy(outs, view, send, recv, i, c):
        return remote(
            view(i, c), outs[i].at[:, head_columns(me)], send.at[i, c], recv.at[i, me], (c, a, w)
        )

    def out_start(outs, view, send, recv, c):
        @pl.when(c == z)
        def _():
            for i in range(2):
                pltpu.make_async_copy(
                    view(i, c), outs[i].at[:, head_columns(me)], recv.at[i, me]
                ).start()

        @pl.when(c != z)
        def _():
            for i in range(2):
                out_copy(outs, view, send, recv, i, c).start()

    def ad_view(i, c):
        return ad_stage.at[i, block_rows(c)]

    def fin_view(i, c):
        return fin_stage.at[i, c]

    ad = (ad_outs, ad_view, ad_send, ad_recv)
    fin = (fin_outs, fin_view, fin_send, fin_recv)

    def back_rows(side, c):
        to = shift_down(a, NA) if side == 0 else shift_up(a, NA)
        return remote(
            row_stage.at[side, :, c],
            row_in.at[side, :, c],
            gr_send.at[side, c],
            gr_recv.at[side, c],
            (z, to, w),
        )

    def back_cols(side, c):
        to = shift_down(w, NW) if side == 0 else shift_up(w, NW)
        return remote(
            col_stage.at[side, :, c],
            col_in.at[side, :, c],
            gc_send.at[side, c],
            gc_recv.at[side, c],
            (z, a, to),
        )

    def compute(g):
        rows = pl.ds(pl.multiple_of(g * GROUP, GROUP), GROUP)
        upstream = qg[1, rows, :]
        pair[0:GROUP, 0:DH] = qg[0, rows, :]
        pair[GROUP : 2 * GROUP, DH : 2 * DH] = upstream
        chunks = jnp.minimum(g, NB - 1) // 2 + 1
        lane = lax.broadcasted_iota(jnp.int32, (1, GROUP), 1)
        pattern = lax.rem(g, 3)

        def both(j):
            duo = pl.ds(2 * j, 2)
            return jnp.concatenate(
                [kv[0, duo].reshape(2 * KEYS, DH), kv[1, duo].reshape(2 * KEYS, DH)], axis=1
            )

        def folded(x, op):
            return op(x.reshape(x.shape[0] // 8, 8, GROUP), axis=0)

        def score_step(j, top):
            r = nt(both(j), pair[...])
            for b in range(2):
                block = 2 * j + b
                causal = jnp.where(lane + (g * GROUP - block * BLOCK) >= 0, 0.0, HIDE).astype(F32)
                live = count[block]
                for f in range(FR):
                    hidden = causal + jnp.where(f < live, 0.0, HIDE).astype(F32)
                    part = slice((b * FR + f) * WIDE, (b * FR + f + 1) * WIDE)
                    s = r[part, 0:GROUP] + (near[pattern] + hidden)
                    scores[j, part, :] = s
                    top = jnp.maximum(top, folded(s, jnp.max))
            pushes[j] = r[:, GROUP:]
            return top

        top = lax.fori_loop(0, chunks, score_step, jnp.full((8, GROUP), HIDE, F32))
        top = jnp.max(top, axis=0, keepdims=True)

        def weight_step(j, carried):
            total, out = carried
            weight = jnp.exp2((scores[j] - top) * (SCALE * LOG2E))
            scores[j] = weight
            return total + folded(weight, jnp.sum), out + mm(kvt[1, j], weight.astype(BF))

        zero = jnp.zeros((DH, GROUP), F32)
        total, out = lax.fori_loop(
            0, chunks, weight_step, (jnp.zeros((8, GROUP), F32), zero)
        )
        total = jnp.sum(total, axis=0, keepdims=True)
        attended = (out / total).astype(BF)
        delta = jnp.sum(
            upstream.T.astype(F32) * attended.astype(F32), axis=0, keepdims=True
        )
        ad_stage[0, rows, :] = attended.T
        inverse = 1.0 / total

        def grad_step(j, grad_q):
            prob = scores[j] * inverse
            slope = (prob * (pushes[j] - delta)).astype(BF)
            acc[j] += mm(jnp.concatenate([slope, prob.astype(BF)], axis=1), pair[...])
            return grad_q + mm(kvt[0, j], slope)

        grad_q = lax.fori_loop(0, chunks, grad_step, zero)
        ad_stage[1, rows, :] = (grad_q * SCALE).astype(BF).T

    def part_of(i):
        return slice(i * DH, (i + 1) * DH)

    def spot(at, low, high):
        return pl.ds(pl.multiple_of(at + low, 8), high - low)

    def rows_out(c):
        for i in range(2):
            for f in range(FR):
                at = lax.rem(c, 2) * KEYS + f * WIDE
                row_stage[0, i, c, f] = acc[c // 2, spot(at, 64, 96), part_of(i)].astype(BF)
                row_stage[1, i, c, f] = acc[c // 2, spot(at, 96, 128), part_of(i)].astype(BF)
        for side in range(2):
            back_rows(side, c).start()

    def cols_out(c):
        spread = picker((64, 64), 1)
        for side in range(2):
            back_rows(side, c).wait_recv()
        for i in range(2):
            for f in range(FR):
                at = lax.rem(c, 2) * KEYS + f * WIDE
                border = jnp.concatenate([row_in[1, i, c, f], row_in[0, i, c, f]], axis=0)
                acc[c // 2, spot(at, 0, 64), part_of(i)] += mm(spread, border)
                col_stage[0, i, c, f] = acc[c // 2, spot(at, 48, 56), part_of(i)].astype(BF)
                col_stage[1, i, c, f] = acc[c // 2, spot(at, 56, 64), part_of(i)].astype(BF)
        for side in range(2):
            back_cols(side, c).start()

    def finish(c):
        for side in range(2):
            back_cols(side, c).wait_recv()
        for i in range(2):
            factor = SCALE if i == 0 else 1.0
            for f in range(FR):
                whole = acc[c // 2, spot(lax.rem(c, 2) * KEYS + f * WIDE, 0, OWN), part_of(i)]
                left = whole[0:8] + col_in[1, i, c, f].astype(F32)
                right = whole[40:48] + col_in[0, i, c, f].astype(F32)
                whole = jnp.concatenate([left, whole[8:40], right], axis=0)
                fin_stage[i, c, f * OWN : (f + 1) * OWN, :] = (whole * factor).astype(BF)
        out_start(*fin, c)

    @pl.when(busy(z))
    def _():
        reach_table(near, radius[me], a, w)
        pair[...] = jnp.zeros_like(pair)
        acc[...] = jnp.zeros_like(acc)
        gather()
        z_sent(KEYS_VALUES, STAGES[3])
        fifth()

        def step(n, _):
            g = NB - n

            @pl.when(g >= 1)
            def _():
                for i in (2, 3):
                    arrived(target(i, g - 1), z_recv.at[i, g - 1])
                    qg[i - 2, block_rows(g - 1), :] = asked[i - 2, g - 1].reshape(BLOCK, DH)

            compute(g)

            @pl.when(g <= NB - 1)
            def _():
                out_start(*ad, g)
                rows_out(g)

            @pl.when(g <= NB - 2)
            def _():
                cols_out(g + 1)

            @pl.when(g <= NB - 3)
            def _():
                finish(g + 2)

            return 0

        lax.fori_loop(0, NB + 1, step, 0)
        cols_out(0)
        finish(1)
        finish(0)

        def drain(c, _):
            for side in range(2):
                col_copy(side, c).wait_send()
                row_copy(side, c).wait_send()
                back_rows(side, c).wait_send()
                back_cols(side, c).wait_send()

            @pl.when(c != z)
            def _():
                for i in range(2):
                    out_copy(*ad, i, c).wait_send()
                    out_copy(*fin, i, c).wait_send()

            return 0

        lax.fori_loop(0, NB, drain, 0)

    z_sent(QUERIES_GRADS, OFFSETS)

    for outs, _, _, recv in (ad, fin):
        for h in range(HEADS):
            for i in range(2):
                arrived(outs[i].at[:, h * DH : (h + 1) * DH], recv.at[i, h])


def write_kernel(*refs):
    flats, tiles, flat, tile, read, write = refs[:4], refs[4:8], *refs[8:]
    reads = [pltpu.make_async_copy(flats[i], flat.at[i], read.at[i]) for i in range(4)]
    writes = [pltpu.make_async_copy(tile.at[i], tiles[i], write.at[i]) for i in range(4)]
    for copy in reads:
        copy.start()
    for i in range(4):
        reads[i].wait()
        tile[i] = flat[i].reshape(tile.shape[1:])
        writes[i].start()
    for copy in writes:
        copy.wait()


def by_columns(array):
    return jnp.transpose(array[0], (0, 2, 1, 3))


def by_rows(array):
    return jnp.transpose(array, (0, 2, 1, 3))[None]


def shards(queries, cache_keys, cache_values, grad_attended, radius, frame_count):
    smem = pl.BlockSpec(memory_space=pltpu.SMEM)
    anywhere = pl.BlockSpec(memory_space=pl.ANY)
    dma = pltpu.SemaphoreType.DMA
    flat = jax.ShapeDtypeStruct((BLOCK, HEADS * DH), BF)
    outs = pl.pallas_call(
        fused_kernel,
        out_shape=(flat,) * 4,
        in_specs=[smem] * 2 + [anywhere] * 4,
        out_specs=(anywhere,) * 4,
        scratch_shapes=[
            pltpu.VMEM((2, NB, FR, 16, TH, DH), BF),
            pltpu.VMEM((2, NB, FR, TW, TH, DH), BF),
            pltpu.VMEM((2, NB, FR, WIDE, DH), BF),
            pltpu.VMEM((2, NB // 2, DH, 2 * KEYS), BF),
            pltpu.VMEM((2, NB * BLOCK, DH), BF),
            pltpu.VMEM((3, WIDE, GROUP), F32),
            pltpu.VMEM((2 * GROUP, 2 * DH), BF),
            pltpu.VMEM((NB // 2, 2 * KEYS, GROUP), F32),
            pltpu.VMEM((NB // 2, 2 * KEYS, GROUP), F32),
            pltpu.VMEM((NB // 2, 2 * KEYS, 2 * DH), F32),
            pltpu.VMEM((2, 2, NB, FR, 32, DH), BF),
            pltpu.VMEM((2, NB * BLOCK, DH), BF),
            pltpu.VMEM((2, 2, NB, FR, 32, DH), BF),
            pltpu.VMEM((2, 2, NB, FR, 32, DH), BF),
            pltpu.VMEM((2, 2, NB, FR, 8, DH), BF),
            pltpu.VMEM((2, 2, NB, FR, 8, DH), BF),
            pltpu.VMEM((2, NB, BLOCK, DH), BF),
            dma((4, NB)),
            dma((4, NB)),
        ]
        + [dma((2, NB))] * 12,
        compiler_params=pltpu.CompilerParams(collective_id=0, has_side_effects=True),
        name="fused",
    )(
        radius,
        frame_count,
        by_columns(cache_keys),
        by_columns(cache_values),
        by_columns(queries),
        by_columns(grad_attended),
    )
    tiles = (FR, TW, TH, HEADS * DH)
    outs = pl.pallas_call(
        write_kernel,
        out_shape=(jax.ShapeDtypeStruct(tiles, BF),) * 4,
        in_specs=[anywhere] * 4,
        out_specs=(anywhere,) * 4,
        scratch_shapes=[
            pltpu.VMEM((4, BLOCK, HEADS * DH), BF),
            pltpu.VMEM((4,) + tiles, BF),
            dma((4,)),
            dma((4,)),
        ],
        name="write",
    )(*outs)
    return tuple(by_rows(x) for x in outs)


def solution(mesh):
    tiled = P("span", None, "ha", "wa", None)
    return jax.shard_map(
        shards,
        mesh=mesh,
        in_specs=(tiled,) * 4 + (P(), P()),
        out_specs=(tiled,) * 4,
        check_vma=False,
    )
```

```python
import math

import jax
import jax.numpy as jnp
from jax import lax
from jax.experimental import pallas as pl
from jax.experimental.pallas import tpu as pltpu
from jax.sharding import PartitionSpec as P

MESH = pl.DeviceIdType.MESH
BF = jnp.bfloat16
F32 = jnp.float32

NB = 8
NA = 8
NW = 4
FR = 3
TH = 4
TW = 12
OWN = TH * TW
WIDE = 128
DH = 128
HEADS = 6
BLOCK = FR * OWN
KEYS = FR * WIDE
GROUP = 128
HIDE = -1e30
SCALE = 1.0 / math.sqrt(DH)
LOG2E = math.log2(math.e)
STAGES = ((4, 1, -1), (3, -3), (2, -2), ())
OFFSETS = (1, -1, 2, -2, 3, -3, 4)
KEYS_VALUES = (0, 1)
QUERIES_GRADS = (2, 3)


def place():
    return lax.axis_index("span"), lax.axis_index("ha"), lax.axis_index("wa")


def busy(z):
    return lax.rem(z, 4) != 3


def head_at(z):
    return z - z // 4


def at_head(h):
    return h + h // 3


def shift_up(i, n):
    return lax.rem(i + 1, n)


def shift_down(i, n):
    return lax.rem(i + n - 1, n)


def greet(z, a, w):
    barrier = pltpu.get_barrier_semaphore()
    for step in range(1, NB):
        pl.semaphore_signal(
            barrier, inc=1, device_id=(lax.rem(z + step, NB), a, w), device_id_type=MESH
        )
    for other in (shift_up(a, NA), shift_down(a, NA)):
        pl.semaphore_signal(barrier, inc=1, device_id=(z, other, w), device_id_type=MESH)
    for other in (shift_up(w, NW), shift_down(w, NW)):
        pl.semaphore_signal(barrier, inc=1, device_id=(z, a, other), device_id_type=MESH)
    pl.semaphore_wait(barrier, NB - 1 + 4)


def picker(shape, edge_dim):
    e = lax.broadcasted_iota(jnp.int32, shape, edge_dim)
    p = lax.broadcasted_iota(jnp.int32, shape, 1 - edge_dim)
    low = e & 31
    wanted = (low >> 1) * 4 + (e >> 5) * 2 + (low & 1)
    return (p == wanted).astype(F32).astype(BF)


def head_columns(h):
    return pl.ds(pl.multiple_of(h * DH, DH), DH)


def remote(src, dst, send, recv, to):
    return pltpu.make_async_remote_copy(
        src_ref=src, dst_ref=dst, send_sem=send, recv_sem=recv, device_id=to, device_id_type=MESH
    )


def nt(x, y):
    return lax.dot_general(x, y, (((1,), (1,)), ((), ())), preferred_element_type=F32)


def mm(x, y):
    return jnp.dot(x, y, preferred_element_type=F32)


def arrived(view, sem):
    pltpu.make_async_copy(view, view, sem).wait()


def reach_table(near, radius, a, w):
    p = lax.broadcasted_iota(jnp.int32, (WIDE, GROUP), 0)
    lane = lax.broadcasted_iota(jnp.int32, (WIDE, GROUP), 1)
    edge = p >= 64
    low = p & 31
    column = jnp.where(edge, low >> 1, p >> 2)
    row = jnp.where(edge, (low & 1) + jnp.where(p >= 96, TH, -2), p & 3)
    column = column - jnp.where(column >= 14, 2, jnp.where(column >= 12, 14, 0))
    full_row, full_column = row + a * TH, column + w * TW
    inside = (full_row >= 0) & (full_row < TH * NA) & (full_column >= 0)
    inside = inside & (full_column < TW * NW)
    for g in range(3):
        spot = lane + (g * GROUP) % OWN
        for _ in range(3):
            spot = jnp.where(spot >= OWN, spot - OWN, spot)
        gap = jnp.maximum(jnp.abs(row - (spot & 3)), jnp.abs(column - (spot >> 2)))
        near[g] = jnp.where((gap <= radius) & inside, 0.0, HIDE).astype(F32)


def fused_kernel(
    radius,
    count,
    k_in,
    v_in,
    q_in,
    g_in,
    att_out,
    dq_out,
    dk_out,
    dv_out,
    wide,
    asked,
    kv,
    kvt,
    qg,
    near,
    pair,
    scores,
    pushes,
    acc,
    edge,
    ad_stage,
    row_stage,
    row_in,
    col_stage,
    col_in,
    fin_stage,
    z_send,
    z_recv,
    c_send,
    c_recv,
    r_send,
    r_recv,
    ad_send,
    ad_recv,
    fin_send,
    fin_recv,
    gr_send,
    gr_recv,
    gc_send,
    gc_recv,
):
    z, a, w = place()
    me = head_at(z)
    arrays = (k_in, v_in, q_in, g_in)
    ad_outs = (att_out, dq_out)
    fin_outs = (dk_out, dv_out)
    greet(z, a, w)

    def block_rows(c):
        return pl.ds(pl.multiple_of(c * BLOCK, 16), BLOCK)

    def target(i, c):
        if i < 2:
            return wide.at[i, c, :, 0:TW]
        return asked.at[i - 2, c]

    def source(i, t):
        return arrays[i].at[:, :, :, head_columns(head_at(t))]

    def z_copy(i, offset, t):
        slot = OFFSETS.index(offset)
        return remote(source(i, t), target(i, z), z_send.at[i, slot], z_recv.at[i, z], (t, a, w))

    def z_local(i):
        return pltpu.make_async_copy(source(i, z), target(i, z), z_recv.at[i, z])

    def z_each(kinds, offsets, act):
        for offset in offsets:
            t = lax.rem(z + offset + NB, NB)

            @pl.when(busy(t))
            def _():
                for i in kinds:
                    act(z_copy(i, offset, t))

    def z_start(kinds, offsets):
        z_each(kinds, offsets, lambda copy: copy.start())

    def z_sent(kinds, offsets):
        z_each(kinds, offsets, lambda copy: copy.wait_send())

    def col_copy(side, c):
        if side == 0:
            src, dst, to = wide.at[:, c, :, 0:2], wide.at[:, c, :, 14:16], shift_down(w, NW)
        else:
            src, dst, to = wide.at[:, c, :, 10:12], wide.at[:, c, :, 12:14], shift_up(w, NW)
        return remote(src, dst, c_send.at[side, c], c_recv.at[side, c], (z, a, to))

    def row_copy(side, c):
        if side == 0:
            dst, to = kv.at[:, c, :, 96:128], shift_down(a, NA)
        else:
            dst, to = kv.at[:, c, :, 64:96], shift_up(a, NA)
        return remote(
            edge.at[side, :, c], dst, r_send.at[side, c], r_recv.at[side, c], (z, to, w)
        )

    upper = z >= NB // 2

    def first():
        @pl.when(busy(z))
        def _():
            for i in range(4):
                z_local(i).start()

        z_start(KEYS_VALUES, STAGES[0])
        z_start(KEYS_VALUES, STAGES[1])

    def second():
        z_sent(KEYS_VALUES, STAGES[0])
        z_start(KEYS_VALUES, STAGES[2])

    def third():
        z_sent(KEYS_VALUES, STAGES[1])
        z_start(KEYS_VALUES, STAGES[3])

    def fourth():
        z_sent(KEYS_VALUES, STAGES[2])

        @pl.when(upper)
        def _():
            z_start(QUERIES_GRADS, OFFSETS)

    def fifth():
        @pl.when(jnp.logical_not(upper))
        def _():
            z_start(QUERIES_GRADS, OFFSETS)

    def gather():
        pick = picker((64, 64), 0)

        def cols_first(c):
            for i in range(2):
                arrived(target(i, c), z_recv.at[i, c])
            for side in range(2):
                col_copy(side, c).start()

        def rows_next(c):
            for side in range(2):
                col_copy(side, c).wait_recv()
            for i in range(2):
                for f in range(FR):
                    tile = wide[i, c, f].reshape(64, DH)
                    kv[i, c, f, 0:64, :] = tile
                    out = mm(pick, tile).astype(BF)
                    edge[0, i, c, f] = out[0:32]
                    edge[1, i, c, f] = out[32:64]
            for side in range(2):
                row_copy(side, c).start()

        def turn(c):
            for side in range(2):
                row_copy(side, c).wait_recv()
            for i in range(2):
                for f in range(FR):
                    kvt[i, c // 2, :, pl.ds(pl.multiple_of(lax.rem(c, 2) * KEYS + f * WIDE, WIDE), WIDE)] = kv[i, c, f].T

        steps = ((0,),) + STAGES
        later = {1: second, 2: third, 3: fourth}
        blocks = [[lax.rem(z + offset + NB, NB) for offset in step] for step in steps]
        for n in range(len(steps) + 2):
            if n < len(steps):
                if n in later:
                    later[n]()
                for c in blocks[n]:
                    cols_first(c)
            if 1 <= n <= len(steps):
                for c in blocks[n - 1]:
                    rows_next(c)
            if n >= 2:
                for c in blocks[n - 2]:
                    turn(c)

    first()

    @pl.when(jnp.logical_not(busy(z)))
    def _():
        second()
        third()
        fourth()
        z_sent(KEYS_VALUES, STAGES[3])
        fifth()

    def out_copy(outs, view, send, recv, i, c):
        return remote(
            view(i, c), outs[i].at[:, head_columns(me)], send.at[i, c], recv.at[i, me], (c, a, w)
        )

    def out_start(outs, view, send, recv, c, kinds=(0, 1)):
        @pl.when(c == z)
        def _():
            for i in kinds:
                pltpu.make_async_copy(
                    view(i, c), outs[i].at[:, head_columns(me)], recv.at[i, me]
                ).start()

        @pl.when(c != z)
        def _():
            for i in kinds:
                out_copy(outs, view, send, recv, i, c).start()

    def ad_view(i, c):
        return ad_stage.at[i, block_rows(c)]

    def fin_view(i, c):
        return fin_stage.at[i, c]

    ad = (ad_outs, ad_view, ad_send, ad_recv)
    fin = (fin_outs, fin_view, fin_send, fin_recv)

    def back_rows(side, c):
        to = shift_down(a, NA) if side == 0 else shift_up(a, NA)
        return remote(
            row_stage.at[side, :, c],
            row_in.at[side, :, c],
            gr_send.at[side, c],
            gr_recv.at[side, c],
            (z, to, w),
        )

    def back_cols(side, c):
        to = shift_down(w, NW) if side == 0 else shift_up(w, NW)
        return remote(
            col_stage.at[side, :, c],
            col_in.at[side, :, c],
            gc_send.at[side, c],
            gc_recv.at[side, c],
            (z, a, to),
        )

    def compute(g):
        rows = pl.ds(pl.multiple_of(g * GROUP, GROUP), GROUP)
        upstream = qg[1, rows, :]
        pair[0:GROUP, 0:DH] = qg[0, rows, :]
        pair[GROUP : 2 * GROUP, DH : 2 * DH] = upstream
        chunks = jnp.minimum(g, NB - 1) // 2 + 1
        lane = lax.broadcasted_iota(jnp.int32, (1, GROUP), 1)
        pattern = lax.rem(g, 3)

        def folded(x, op):
            return op(x.reshape(x.shape[0] // 8, 8, GROUP), axis=0)

        def score_step(j, top):
            duo = pl.ds(2 * j, 2)
            r = nt(kv[0, duo].reshape(2 * KEYS, DH), pair[0:GROUP, 0:DH])
            for b in range(2):
                block = 2 * j + b
                causal = jnp.where(lane + (g * GROUP - block * BLOCK) >= 0, 0.0, HIDE).astype(F32)
                live = count[block]
                for f in range(FR):
                    hidden = causal + jnp.where(f < live, 0.0, HIDE).astype(F32)
                    part = slice((b * FR + f) * WIDE, (b * FR + f + 1) * WIDE)
                    s = r[part, :] + (near[pattern] + hidden)
                    scores[j, part, :] = s
                    top = jnp.maximum(top, folded(s, jnp.max))
            pushes[j] = nt(kv[1, duo].reshape(2 * KEYS, DH), pair[GROUP:, DH:])
            return top

        top = lax.fori_loop(0, chunks, score_step, jnp.full((8, GROUP), HIDE, F32))
        top = jnp.max(top, axis=0, keepdims=True)

        def weight_step(j, carried):
            total, out = carried
            weight = jnp.exp2((scores[j] - top) * (SCALE * LOG2E))
            scores[j] = weight
            return total + folded(weight, jnp.sum), out + mm(kvt[1, j], weight.astype(BF))

        zero = jnp.zeros((DH, GROUP), F32)
        total, out = lax.fori_loop(
            0, chunks, weight_step, (jnp.zeros((8, GROUP), F32), zero)
        )
        total = jnp.sum(total, axis=0, keepdims=True)
        attended = (out / total).astype(BF)
        delta = jnp.sum(
            upstream.T.astype(F32) * attended.astype(F32), axis=0, keepdims=True
        )
        ad_stage[0, rows, :] = attended.T
        inverse = 1.0 / total

        @pl.when(g <= NB - 1)
        def _():
            out_start(*ad, g, (0,))


        def grad_step(j, grad_q):
            prob = scores[j] * inverse
            slope = (prob * (pushes[j] - delta)).astype(BF)
            acc[j, :, 0:DH] += mm(slope, pair[0:GROUP, 0:DH])
            acc[j, :, DH:] += mm(prob.astype(BF), pair[GROUP:, DH:])
            return grad_q + mm(kvt[0, j], slope)

        grad_q = lax.fori_loop(0, chunks, grad_step, zero)
        ad_stage[1, rows, :] = (grad_q * SCALE).astype(BF).T

    def part_of(i):
        return slice(i * DH, (i + 1) * DH)

    def spot(at, low, high):
        return pl.ds(pl.multiple_of(at + low, 8), high - low)

    def rows_out(c):
        for i in range(2):
            for f in range(FR):
                at = lax.rem(c, 2) * KEYS + f * WIDE
                row_stage[0, i, c, f] = acc[c // 2, spot(at, 64, 96), part_of(i)].astype(BF)
                row_stage[1, i, c, f] = acc[c // 2, spot(at, 96, 128), part_of(i)].astype(BF)
        for side in range(2):
            back_rows(side, c).start()

    def cols_out(c):
        spread = picker((64, 64), 1)
        for side in range(2):
            back_rows(side, c).wait_recv()
        for i in range(2):
            for f in range(FR):
                at = lax.rem(c, 2) * KEYS + f * WIDE
                border = jnp.concatenate([row_in[1, i, c, f], row_in[0, i, c, f]], axis=0)
                acc[c // 2, spot(at, 0, 64), part_of(i)] += mm(spread, border)
                col_stage[0, i, c, f] = acc[c // 2, spot(at, 48, 56), part_of(i)].astype(BF)
                col_stage[1, i, c, f] = acc[c // 2, spot(at, 56, 64), part_of(i)].astype(BF)
        for side in range(2):
            back_cols(side, c).start()

    def finish(c):
        for side in range(2):
            back_cols(side, c).wait_recv()
        for i in range(2):
            factor = SCALE if i == 0 else 1.0
            for f in range(FR):
                whole = acc[c // 2, spot(lax.rem(c, 2) * KEYS + f * WIDE, 0, OWN), part_of(i)]
                left = whole[0:8] + col_in[1, i, c, f].astype(F32)
                right = whole[40:48] + col_in[0, i, c, f].astype(F32)
                whole = jnp.concatenate([left, whole[8:40], right], axis=0)
                fin_stage[i, c, f * OWN : (f + 1) * OWN, :] = (whole * factor).astype(BF)
        out_start(*fin, c)

    @pl.when(busy(z))
    def _():
        reach_table(near, radius[me], a, w)
        pair[...] = jnp.zeros_like(pair)
        acc[...] = jnp.zeros_like(acc)
        gather()
        z_sent(KEYS_VALUES, STAGES[3])
        fifth()

        def step(n, _):
            g = NB - n

            @pl.when(g >= 1)
            def _():
                for i in (2, 3):
                    arrived(target(i, g - 1), z_recv.at[i, g - 1])
                    qg[i - 2, block_rows(g - 1), :] = asked[i - 2, g - 1].reshape(BLOCK, DH)

            compute(g)

            @pl.when(g <= NB - 1)
            def _():
                out_start(*ad, g, (1,))
                rows_out(g)

            @pl.when(g <= NB - 2)
            def _():
                cols_out(g + 1)

            @pl.when(g <= NB - 3)
            def _():
                finish(g + 2)

            return 0

        lax.fori_loop(0, NB + 1, step, 0)
        cols_out(0)
        finish(1)
        finish(0)

        def drain(c, _):
            for side in range(2):
                col_copy(side, c).wait_send()
                row_copy(side, c).wait_send()
                back_rows(side, c).wait_send()
                back_cols(side, c).wait_send()

            @pl.when(c != z)
            def _():
                for i in range(2):
                    out_copy(*ad, i, c).wait_send()
                    out_copy(*fin, i, c).wait_send()

            return 0

        lax.fori_loop(0, NB, drain, 0)

    z_sent(QUERIES_GRADS, OFFSETS)

    for outs, _, _, recv in (ad, fin):
        for h in range(HEADS):
            for i in range(2):
                arrived(outs[i].at[:, h * DH : (h + 1) * DH], recv.at[i, h])


def write_kernel(*refs):
    flats, tiles, flat, tile, read, write = refs[:4], refs[4:8], *refs[8:]
    reads = [pltpu.make_async_copy(flats[i], flat.at[i], read.at[i]) for i in range(4)]
    writes = [pltpu.make_async_copy(tile.at[i], tiles[i], write.at[i]) for i in range(4)]
    for copy in reads:
        copy.start()
    for i in range(4):
        reads[i].wait()
        tile[i] = flat[i].reshape(tile.shape[1:])
        writes[i].start()
    for copy in writes:
        copy.wait()


def by_columns(array):
    return jnp.transpose(array[0], (0, 2, 1, 3))


def by_rows(array):
    return jnp.transpose(array, (0, 2, 1, 3))[None]


def shards(queries, cache_keys, cache_values, grad_attended, radius, frame_count):
    smem = pl.BlockSpec(memory_space=pltpu.SMEM)
    anywhere = pl.BlockSpec(memory_space=pl.ANY)
    dma = pltpu.SemaphoreType.DMA
    flat = jax.ShapeDtypeStruct((BLOCK, HEADS * DH), BF)
    outs = pl.pallas_call(
        fused_kernel,
        out_shape=(flat,) * 4,
        in_specs=[smem] * 2 + [anywhere] * 4,
        out_specs=(anywhere,) * 4,
        scratch_shapes=[
            pltpu.VMEM((2, NB, FR, 16, TH, DH), BF),
            pltpu.VMEM((2, NB, FR, TW, TH, DH), BF),
            pltpu.VMEM((2, NB, FR, WIDE, DH), BF),
            pltpu.VMEM((2, NB // 2, DH, 2 * KEYS), BF),
            pltpu.VMEM((2, NB * BLOCK, DH), BF),
            pltpu.VMEM((3, WIDE, GROUP), F32),
            pltpu.VMEM((2 * GROUP, 2 * DH), BF),
            pltpu.VMEM((NB // 2, 2 * KEYS, GROUP), F32),
            pltpu.VMEM((NB // 2, 2 * KEYS, GROUP), F32),
            pltpu.VMEM((NB // 2, 2 * KEYS, 2 * DH), F32),
            pltpu.VMEM((2, 2, NB, FR, 32, DH), BF),
            pltpu.VMEM((2, NB * BLOCK, DH), BF),
            pltpu.VMEM((2, 2, NB, FR, 32, DH), BF),
            pltpu.VMEM((2, 2, NB, FR, 32, DH), BF),
            pltpu.VMEM((2, 2, NB, FR, 8, DH), BF),
            pltpu.VMEM((2, 2, NB, FR, 8, DH), BF),
            pltpu.VMEM((2, NB, BLOCK, DH), BF),
            dma((4, NB)),
            dma((4, NB)),
        ]
        + [dma((2, NB))] * 12,
        compiler_params=pltpu.CompilerParams(collective_id=0, has_side_effects=True),
        name="fused",
    )(
        radius,
        frame_count,
        by_columns(cache_keys),
        by_columns(cache_values),
        by_columns(queries),
        by_columns(grad_attended),
    )
    tiles = (FR, TW, TH, HEADS * DH)
    outs = pl.pallas_call(
        write_kernel,
        out_shape=(jax.ShapeDtypeStruct(tiles, BF),) * 4,
        in_specs=[anywhere] * 4,
        out_specs=(anywhere,) * 4,
        scratch_shapes=[
            pltpu.VMEM((4, BLOCK, HEADS * DH), BF),
            pltpu.VMEM((4,) + tiles, BF),
            dma((4,)),
            dma((4,)),
        ],
        name="write",
    )(*outs)
    return tuple(by_rows(x) for x in outs)


def solution(mesh):
    tiled = P("span", None, "ha", "wa", None)
    return jax.shard_map(
        shards,
        mesh=mesh,
        in_specs=(tiled,) * 4 + (P(), P()),
        out_specs=(tiled,) * 4,
        check_vma=False,
    )
```

```python
import math

import jax
import jax.numpy as jnp
from jax import lax
from jax.experimental import pallas as pl
from jax.experimental.pallas import tpu as pltpu
from jax.sharding import PartitionSpec as P

MESH = pl.DeviceIdType.MESH
BF = jnp.bfloat16
F32 = jnp.float32

NB = 8
NA = 8
NW = 4
FR = 3
TH = 4
TW = 12
OWN = TH * TW
WIDE = 128
DH = 128
HEADS = 6
BLOCK = FR * OWN
KEYS = FR * WIDE
GROUP = 128
HIDE = -1e30
SCALE = 1.0 / math.sqrt(DH)
LOG2E = math.log2(math.e)
STAGES = ((4, 1, -1), (3, -3), (2, -2), ())
OFFSETS = (1, -1, 2, -2, 3, -3, 4)
KEYS_VALUES = (0, 1)
QUERIES_GRADS = (2, 3)


def place():
    return lax.axis_index("span"), lax.axis_index("ha"), lax.axis_index("wa")


def busy(z):
    return lax.rem(z, 4) != 3


def head_at(z):
    return z - z // 4


def at_head(h):
    return h + h // 3


def shift_up(i, n):
    return lax.rem(i + 1, n)


def shift_down(i, n):
    return lax.rem(i + n - 1, n)


def greet(z, a, w):
    barrier = pltpu.get_barrier_semaphore()
    for step in range(1, NB):
        pl.semaphore_signal(
            barrier, inc=1, device_id=(lax.rem(z + step, NB), a, w), device_id_type=MESH
        )
    for other in (shift_up(a, NA), shift_down(a, NA)):
        pl.semaphore_signal(barrier, inc=1, device_id=(z, other, w), device_id_type=MESH)
    for other in (shift_up(w, NW), shift_down(w, NW)):
        pl.semaphore_signal(barrier, inc=1, device_id=(z, a, other), device_id_type=MESH)
    pl.semaphore_wait(barrier, NB - 1 + 4)


def picker(shape, edge_dim):
    e = lax.broadcasted_iota(jnp.int32, shape, edge_dim)
    p = lax.broadcasted_iota(jnp.int32, shape, 1 - edge_dim)
    low = e & 31
    wanted = (low >> 1) * 4 + (e >> 5) * 2 + (low & 1)
    return (p == wanted).astype(F32).astype(BF)


def head_columns(h):
    return pl.ds(pl.multiple_of(h * DH, DH), DH)


def remote(src, dst, send, recv, to):
    return pltpu.make_async_remote_copy(
        src_ref=src, dst_ref=dst, send_sem=send, recv_sem=recv, device_id=to, device_id_type=MESH
    )


def nt(x, y):
    return lax.dot_general(x, y, (((1,), (1,)), ((), ())), preferred_element_type=F32)


def mm(x, y):
    return jnp.dot(x, y, preferred_element_type=F32)


def arrived(view, sem):
    pltpu.make_async_copy(view, view, sem).wait()


def reach_table(near, radius, a, w):
    p = lax.broadcasted_iota(jnp.int32, (WIDE, GROUP), 0)
    lane = lax.broadcasted_iota(jnp.int32, (WIDE, GROUP), 1)
    edge = p >= 64
    low = p & 31
    column = jnp.where(edge, low >> 1, p >> 2)
    row = jnp.where(edge, (low & 1) + jnp.where(p >= 96, TH, -2), p & 3)
    column = column - jnp.where(column >= 14, 2, jnp.where(column >= 12, 14, 0))
    full_row, full_column = row + a * TH, column + w * TW
    inside = (full_row >= 0) & (full_row < TH * NA) & (full_column >= 0)
    inside = inside & (full_column < TW * NW)
    for g in range(3):
        spot = lane + (g * GROUP) % OWN
        for _ in range(3):
            spot = jnp.where(spot >= OWN, spot - OWN, spot)
        gap = jnp.maximum(jnp.abs(row - (spot & 3)), jnp.abs(column - (spot >> 2)))
        near[g] = jnp.where((gap <= radius) & inside, 0.0, HIDE).astype(F32)


def fused_kernel(
    radius,
    count,
    k_in,
    v_in,
    q_in,
    g_in,
    att_out,
    dq_out,
    dk_out,
    dv_out,
    wide,
    asked,
    kv,
    kvt,
    qg,
    near,
    pair,
    scores,
    pushes,
    acc,
    edge,
    ad_stage,
    row_stage,
    row_in,
    col_stage,
    col_in,
    fin_stage,
    z_send,
    z_recv,
    c_send,
    c_recv,
    r_send,
    r_recv,
    ad_send,
    ad_recv,
    fin_send,
    fin_recv,
    gr_send,
    gr_recv,
    gc_send,
    gc_recv,
):
    z, a, w = place()
    me = head_at(z)
    arrays = (k_in, v_in, q_in, g_in)
    ad_outs = (att_out, dq_out)
    fin_outs = (dk_out, dv_out)
    greet(z, a, w)

    def block_rows(c):
        return pl.ds(pl.multiple_of(c * BLOCK, 16), BLOCK)

    def target(i, c):
        if i < 2:
            return wide.at[i, c, :, 0:TW]
        return asked.at[i - 2, c]

    def source(i, t):
        return arrays[i].at[:, :, :, head_columns(head_at(t))]

    def z_copy(i, offset, t):
        slot = OFFSETS.index(offset)
        return remote(source(i, t), target(i, z), z_send.at[i, slot], z_recv.at[i, z], (t, a, w))

    def z_local(i):
        return pltpu.make_async_copy(source(i, z), target(i, z), z_recv.at[i, z])

    def z_each(kinds, offsets, act):
        for offset in offsets:
            t = lax.rem(z + offset + NB, NB)

            @pl.when(busy(t))
            def _():
                for i in kinds:
                    act(z_copy(i, offset, t))

    def z_start(kinds, offsets):
        z_each(kinds, offsets, lambda copy: copy.start())

    def z_sent(kinds, offsets):
        z_each(kinds, offsets, lambda copy: copy.wait_send())

    def col_copy(side, c):
        if side == 0:
            src, dst, to = wide.at[:, c, :, 0:2], wide.at[:, c, :, 14:16], shift_down(w, NW)
        else:
            src, dst, to = wide.at[:, c, :, 10:12], wide.at[:, c, :, 12:14], shift_up(w, NW)
        return remote(src, dst, c_send.at[side, c], c_recv.at[side, c], (z, a, to))

    def row_copy(side, c):
        if side == 0:
            dst, to = kv.at[:, c, :, 96:128], shift_down(a, NA)
        else:
            dst, to = kv.at[:, c, :, 64:96], shift_up(a, NA)
        return remote(
            edge.at[side, :, c], dst, r_send.at[side, c], r_recv.at[side, c], (z, to, w)
        )

    upper = z >= NB // 2

    def first():
        @pl.when(busy(z))
        def _():
            for i in range(4):
                z_local(i).start()

        z_start(KEYS_VALUES, STAGES[0])
        z_start(KEYS_VALUES, STAGES[1])

    def second():
        z_sent(KEYS_VALUES, STAGES[0])
        z_start(KEYS_VALUES, STAGES[2])

    def third():
        z_sent(KEYS_VALUES, STAGES[1])
        z_start(KEYS_VALUES, STAGES[3])

    def fourth():
        z_sent(KEYS_VALUES, STAGES[2])

        @pl.when(upper)
        def _():
            z_start(QUERIES_GRADS, OFFSETS)

    def fifth():
        @pl.when(jnp.logical_not(upper))
        def _():
            z_start(QUERIES_GRADS, OFFSETS)

    def gather():
        pick = picker((64, 64), 0)

        def cols_first(c):
            for i in range(2):
                arrived(target(i, c), z_recv.at[i, c])
            for side in range(2):
                col_copy(side, c).start()

        def rows_next(c):
            for side in range(2):
                col_copy(side, c).wait_recv()
            for i in range(2):
                for f in range(FR):
                    tile = wide[i, c, f].reshape(64, DH)
                    kv[i, c, f, 0:64, :] = tile
                    out = mm(pick, tile).astype(BF)
                    edge[0, i, c, f] = out[0:32]
                    edge[1, i, c, f] = out[32:64]
            for side in range(2):
                row_copy(side, c).start()

        def turn(c):
            for side in range(2):
                row_copy(side, c).wait_recv()
            for i in range(2):
                for f in range(FR):
                    kvt[i, c // 2, :, pl.ds(pl.multiple_of(lax.rem(c, 2) * KEYS + f * WIDE, WIDE), WIDE)] = kv[i, c, f].T

        steps = ((0,),) + STAGES
        later = {1: second, 2: third, 3: fourth}
        blocks = [[lax.rem(z + offset + NB, NB) for offset in step] for step in steps]
        for n in range(len(steps) + 2):
            if n < len(steps):
                if n in later:
                    later[n]()
                for c in blocks[n]:
                    cols_first(c)
            if 1 <= n <= len(steps):
                for c in blocks[n - 1]:
                    rows_next(c)
            if n >= 2:
                for c in blocks[n - 2]:
                    turn(c)

    first()

    @pl.when(jnp.logical_not(busy(z)))
    def _():
        second()
        third()
        fourth()
        z_sent(KEYS_VALUES, STAGES[3])
        fifth()

    def out_copy(outs, view, send, recv, i, c):
        return remote(
            view(i, c), outs[i].at[:, head_columns(me)], send.at[i, c], recv.at[i, me], (c, a, w)
        )

    def out_start(outs, view, send, recv, c, kinds=(0, 1)):
        @pl.when(c == z)
        def _():
            for i in kinds:
                pltpu.make_async_copy(
                    view(i, c), outs[i].at[:, head_columns(me)], recv.at[i, me]
                ).start()

        @pl.when(c != z)
        def _():
            for i in kinds:
                out_copy(outs, view, send, recv, i, c).start()

    def ad_view(i, c):
        return ad_stage.at[i, block_rows(c)]

    def fin_view(i, c):
        return fin_stage.at[i, c]

    ad = (ad_outs, ad_view, ad_send, ad_recv)
    fin = (fin_outs, fin_view, fin_send, fin_recv)

    def back_rows(side, c):
        to = shift_down(a, NA) if side == 0 else shift_up(a, NA)
        return remote(
            row_stage.at[side, :, c],
            row_in.at[side, :, c],
            gr_send.at[side, c],
            gr_recv.at[side, c],
            (z, to, w),
        )

    def back_cols(side, c):
        to = shift_down(w, NW) if side == 0 else shift_up(w, NW)
        return remote(
            col_stage.at[side, :, c],
            col_in.at[side, :, c],
            gc_send.at[side, c],
            gc_recv.at[side, c],
            (z, a, to),
        )

    def compute(g):
        rows = pl.ds(pl.multiple_of(g * GROUP, GROUP), GROUP)
        upstream = qg[1, rows, :]
        pair[0:GROUP, 0:DH] = qg[0, rows, :]
        pair[GROUP : 2 * GROUP, DH : 2 * DH] = upstream
        chunks = jnp.minimum(g, NB - 1) // 2 + 1
        lane = lax.broadcasted_iota(jnp.int32, (1, GROUP), 1)
        pattern = lax.rem(g, 3)

        def folded(x, op):
            return op(x.reshape(x.shape[0] // 8, 8, GROUP), axis=0)

        def score_step(j, top):
            duo = pl.ds(2 * j, 2)
            r = nt(kv[0, duo].reshape(2 * KEYS, DH), pair[0:GROUP, 0:DH])
            for b in range(2):
                block = 2 * j + b
                causal = jnp.where(lane + (g * GROUP - block * BLOCK) >= 0, 0.0, HIDE).astype(F32)
                live = count[block]
                for f in range(FR):
                    hidden = causal + jnp.where(f < live, 0.0, HIDE).astype(F32)
                    part = slice((b * FR + f) * WIDE, (b * FR + f + 1) * WIDE)
                    s = r[part, :] + (near[pattern] + hidden)
                    scores[j, part, :] = s
                    top = jnp.maximum(top, folded(s, jnp.max))
            pushes[j] = nt(kv[1, duo].reshape(2 * KEYS, DH), pair[GROUP:, DH:])
            return top

        top = lax.fori_loop(0, chunks, score_step, jnp.full((8, GROUP), HIDE, F32))
        top = jnp.max(top, axis=0, keepdims=True)

        def weight_step(j, carried):
            total, out = carried
            weight = jnp.exp2((scores[j] - top) * (SCALE * LOG2E))
            scores[j] = weight
            return total + folded(weight, jnp.sum), out + mm(kvt[1, j], weight.astype(BF))

        zero = jnp.zeros((DH, GROUP), F32)
        total, out = lax.fori_loop(
            0, chunks, weight_step, (jnp.zeros((8, GROUP), F32), zero)
        )
        total = jnp.sum(total, axis=0, keepdims=True)
        attended = (out / total).astype(BF)
        delta = jnp.sum(
            upstream.T.astype(F32) * attended.astype(F32), axis=0, keepdims=True
        )
        ad_stage[0, rows, :] = attended.T
        inverse = 1.0 / total

        @pl.when(g <= NB - 1)
        def _():
            out_start(*ad, g, (0,))


        def grad_step(j, grad_q):
            prob = scores[j] * inverse
            slope = (prob * (pushes[j] - delta)).astype(BF)
            acc[j, :, 0:DH] += mm(slope, pair[0:GROUP, 0:DH])
            acc[j, :, DH:] += mm(prob.astype(BF), pair[GROUP:, DH:])
            return grad_q + mm(kvt[0, j], slope)

        grad_q = lax.fori_loop(0, chunks, grad_step, zero)
        ad_stage[1, rows, :] = (grad_q * SCALE).astype(BF).T

    def part_of(i):
        return slice(i * DH, (i + 1) * DH)

    def spot(at, low, high):
        return pl.ds(pl.multiple_of(at + low, 8), high - low)

    def rows_out(c):
        for i in range(2):
            for f in range(FR):
                at = lax.rem(c, 2) * KEYS + f * WIDE
                row_stage[0, i, c, f] = acc[c // 2, spot(at, 64, 96), part_of(i)].astype(BF)
                row_stage[1, i, c, f] = acc[c // 2, spot(at, 96, 128), part_of(i)].astype(BF)
        for side in range(2):
            back_rows(side, c).start()

    def cols_out(c):
        spread = picker((64, 64), 1)
        for side in range(2):
            back_rows(side, c).wait_recv()
        for i in range(2):
            for f in range(FR):
                at = lax.rem(c, 2) * KEYS + f * WIDE
                border = jnp.concatenate([row_in[1, i, c, f], row_in[0, i, c, f]], axis=0)
                acc[c // 2, spot(at, 0, 64), part_of(i)] += mm(spread, border)
                col_stage[0, i, c, f] = acc[c // 2, spot(at, 48, 56), part_of(i)].astype(BF)
                col_stage[1, i, c, f] = acc[c // 2, spot(at, 56, 64), part_of(i)].astype(BF)
        for side in range(2):
            back_cols(side, c).start()

    def finish(c):
        for side in range(2):
            back_cols(side, c).wait_recv()
        for i in range(2):
            factor = SCALE if i == 0 else 1.0
            for f in range(FR):
                whole = acc[c // 2, spot(lax.rem(c, 2) * KEYS + f * WIDE, 0, OWN), part_of(i)]
                left = whole[0:8] + col_in[1, i, c, f].astype(F32)
                right = whole[40:48] + col_in[0, i, c, f].astype(F32)
                whole = jnp.concatenate([left, whole[8:40], right], axis=0)
                fin_stage[i, c, f * OWN : (f + 1) * OWN, :] = (whole * factor).astype(BF)
        out_start(*fin, c)

    @pl.when(busy(z))
    def _():
        reach_table(near, radius[me], a, w)
        pair[...] = jnp.zeros_like(pair)
        acc[...] = jnp.zeros_like(acc)
        gather()
        z_sent(KEYS_VALUES, STAGES[3])
        fifth()

        def step(n, _):
            g = NB - n

            @pl.when(g >= 1)
            def _():
                for i in (2, 3):
                    arrived(target(i, g - 1), z_recv.at[i, g - 1])
                    qg[i - 2, block_rows(g - 1), :] = asked[i - 2, g - 1].reshape(BLOCK, DH)

            compute(g)

            @pl.when(g <= NB - 1)
            def _():
                out_start(*ad, g, (1,))
                rows_out(g)

            @pl.when(g <= NB - 2)
            def _():
                cols_out(g + 1)

            @pl.when(g <= NB - 4)
            def _():
                finish(g + 3)

            return 0

        lax.fori_loop(0, NB + 1, step, 0)
        finish(2)
        cols_out(0)
        finish(1)
        finish(0)

        def drain(c, _):
            for side in range(2):
                col_copy(side, c).wait_send()
                row_copy(side, c).wait_send()
                back_rows(side, c).wait_send()
                back_cols(side, c).wait_send()

            @pl.when(c != z)
            def _():
                for i in range(2):
                    out_copy(*ad, i, c).wait_send()
                    out_copy(*fin, i, c).wait_send()

            return 0

        lax.fori_loop(0, NB, drain, 0)

    z_sent(QUERIES_GRADS, OFFSETS)

    for outs, _, _, recv in (ad, fin):
        for h in range(HEADS):
            for i in range(2):
                arrived(outs[i].at[:, h * DH : (h + 1) * DH], recv.at[i, h])


def write_kernel(*refs):
    flats, tiles, flat, tile, read, write = refs[:4], refs[4:8], *refs[8:]
    reads = [pltpu.make_async_copy(flats[i], flat.at[i], read.at[i]) for i in range(4)]
    writes = [pltpu.make_async_copy(tile.at[i], tiles[i], write.at[i]) for i in range(4)]
    for copy in reads:
        copy.start()
    for i in range(4):
        reads[i].wait()
        tile[i] = flat[i].reshape(tile.shape[1:])
        writes[i].start()
    for copy in writes:
        copy.wait()


def by_columns(array):
    return jnp.transpose(array[0], (0, 2, 1, 3))


def by_rows(array):
    return jnp.transpose(array, (0, 2, 1, 3))[None]


def shards(queries, cache_keys, cache_values, grad_attended, radius, frame_count):
    smem = pl.BlockSpec(memory_space=pltpu.SMEM)
    anywhere = pl.BlockSpec(memory_space=pl.ANY)
    dma = pltpu.SemaphoreType.DMA
    flat = jax.ShapeDtypeStruct((BLOCK, HEADS * DH), BF)
    outs = pl.pallas_call(
        fused_kernel,
        out_shape=(flat,) * 4,
        in_specs=[smem] * 2 + [anywhere] * 4,
        out_specs=(anywhere,) * 4,
        scratch_shapes=[
            pltpu.VMEM((2, NB, FR, 16, TH, DH), BF),
            pltpu.VMEM((2, NB, FR, TW, TH, DH), BF),
            pltpu.VMEM((2, NB, FR, WIDE, DH), BF),
            pltpu.VMEM((2, NB // 2, DH, 2 * KEYS), BF),
            pltpu.VMEM((2, NB * BLOCK, DH), BF),
            pltpu.VMEM((3, WIDE, GROUP), F32),
            pltpu.VMEM((2 * GROUP, 2 * DH), BF),
            pltpu.VMEM((NB // 2, 2 * KEYS, GROUP), F32),
            pltpu.VMEM((NB // 2, 2 * KEYS, GROUP), F32),
            pltpu.VMEM((NB // 2, 2 * KEYS, 2 * DH), F32),
            pltpu.VMEM((2, 2, NB, FR, 32, DH), BF),
            pltpu.VMEM((2, NB * BLOCK, DH), BF),
            pltpu.VMEM((2, 2, NB, FR, 32, DH), BF),
            pltpu.VMEM((2, 2, NB, FR, 32, DH), BF),
            pltpu.VMEM((2, 2, NB, FR, 8, DH), BF),
            pltpu.VMEM((2, 2, NB, FR, 8, DH), BF),
            pltpu.VMEM((2, NB, BLOCK, DH), BF),
            dma((4, NB)),
            dma((4, NB)),
        ]
        + [dma((2, NB))] * 12,
        compiler_params=pltpu.CompilerParams(collective_id=0, has_side_effects=True),
        name="fused",
    )(
        radius,
        frame_count,
        by_columns(cache_keys),
        by_columns(cache_values),
        by_columns(queries),
        by_columns(grad_attended),
    )
    tiles = (FR, TW, TH, HEADS * DH)
    outs = pl.pallas_call(
        write_kernel,
        out_shape=(jax.ShapeDtypeStruct(tiles, BF),) * 4,
        in_specs=[anywhere] * 4,
        out_specs=(anywhere,) * 4,
        scratch_shapes=[
            pltpu.VMEM((4, BLOCK, HEADS * DH), BF),
            pltpu.VMEM((4,) + tiles, BF),
            dma((4,)),
            dma((4,)),
        ],
        name="write",
    )(*outs)
    return tuple(by_rows(x) for x in outs)


def solution(mesh):
    tiled = P("span", None, "ha", "wa", None)
    return jax.shard_map(
        shards,
        mesh=mesh,
        in_specs=(tiled,) * 4 + (P(), P()),
        out_specs=(tiled,) * 4,
        check_vma=False,
    )
```
